256 devices in a mesh: section: 2 (over z_lo), seq: 32 (over x, z_hi, core), tp: 4 (over y).
Axes of the slice: x: 4, y: 4, z: 8 (z_hi: 4, z_lo: 2; z = z_hi * 2 + z_lo), core: 2. Of those that a mesh axis runs over, the one named last changes fastest.
Arguments:
- hidden: bfloat16 [1024, 3072], P('seq', 'tp'), may hold values from -6 to 6
- qkv_weight: bfloat16 [2, 3072, 3, 1536], P('section', None, None, 'tp'), may hold values from -0.109375 to 0.109375
- qk_gain: float32 [2, 2, 64], P('section'), may hold values from 1.3 to 2
- out_weight: bfloat16 [2, 1536, 3072], P('section', 'tp'), may hold values from -0.15625 to 0.15625
- mod_weight: bfloat16 [2, 512, 18432], P('section', None, ('seq', 'tp')), may hold values from -0.5 to 0.5
- stale_kv: bfloat16 [2, 2, 1024, 1536], P('section', None, 'seq', 'tp'), may hold values from -600 to 600
- patch_lengths: int32 [4], replicated, may hold values from 1 to 399, 798 in all
- positions: int32 [3, 1024], P(None, 'seq'), may hold values from 0 to 44, as said below
- timestep: int32 [1], replicated, may hold values from 0 to 999
Outputs:
- hidden_out: bfloat16 [2, 1024, 3072], P('section', 'seq', 'tp')
- fresh_kv: bfloat16 [2, 2, 1024, 1536], P('section', None, 'seq', 'tp')
The draws below stay inside these ranges and needn't reach their ends.
Inputs may be any that keep to these rules, and one draw needn't show every extreme that they name: `patch_lengths`: the 4 counts sum to 798, the largest exactly (798) // 2. `positions`: frames lie below 13, rows below 30, columns below 45.
All inputs are finite; a program needn't handle non-finite values.
Results may differ from the reference program's by a relative error of at most 0.025.
Values may be sent and summed in bfloat16 or wider, within the bound.
A program may use at most 64 MiB of HBM per device.

```python
import math
import jax
import jax.numpy as jnp
import numpy as np
from jax import lax

D = 3072
HEAD = 64
TEMB = 512
HEADS = 24
TEXT = 226
NPATCH = 4
LAYERS = 2
TOKENS = 1024
HD = 1536


def draw_stale_kv(key, part):
    full_shape = (LAYERS, 2, TOKENS, HEADS * HEAD)
    key_one = jax.random.fold_in(key, 0)
    baseline = jax.random.normal(key_one, full_shape, jnp.float32)
    result = baseline * jnp.array([1.6, 1.0], jnp.float32)[None, :, None, None]
    return result.astype(jnp.bfloat16)


def draw_positions(key, part):
    key_one, key_two, key_three = jax.random.split(key, 3)
    frames = jax.random.randint(key_one, (TOKENS,), 0, 13)
    grid_rows = jax.random.randint(key_two, (TOKENS,), 0, 30)
    grid_cols = jax.random.randint(key_three, (TOKENS,), 0, 45)
    grid_cols = grid_cols.at[TOKENS - 1].set(44)
    frames = frames.at[0].set(0)
    return jnp.stack([frames, grid_rows, grid_cols]).astype(jnp.int32)


def block_scale(key, dims, cuts, least, largest):
    factor_of = 1.0
    for position, blocks in cuts:
        steps = jax.random.uniform(jax.random.fold_in(jax.random.fold_in(key, 6), position), (blocks,), jnp.float32, least / len(cuts), largest / len(cuts))
        factor_of = factor_of * jnp.repeat(jnp.exp(steps), dims[position] // blocks).reshape((-1,) + (1,) * (len(dims) - 1 - position))
    return factor_of


def length_profile(amount, total, limit, slope):
    weights = [(1 << 20) // math.isqrt(standing ** slope) + 1 for standing in range(2, amount + 1)]
    rest, given = total - limit - (amount - 1), [1] * (amount - 1)
    while rest > 0:
        candidates = [i for i in range(amount - 1) if given[i] < limit]
        pool, remaining = sum([weights[i] for i in candidates]), rest
        for i in candidates:
            extra = min(limit - given[i], max(1, remaining * weights[i] // pool), rest)
            given[i] = given[i] + extra
            rest = rest - extra
    return np.array([limit] + given)


def ragged_sizes(rng, count, total, limit, skew):
    if count == 2:
        one = jax.random.randint(rng, (), max(1, total - limit), min(limit, total - 1) + 1)
        return jnp.stack([one, total - one])
    tallies = jnp.asarray(length_profile(count, total, limit, skew), jnp.int32)
    couples = (count - 1) // 2
    giver, receiver = tallies[1:1 + 2 * couples:2], tallies[2:2 + 2 * couples:2]
    margin = jnp.minimum(giver - 1, limit - receiver)
    moved = jax.random.randint(jax.random.fold_in(rng, 1), (couples,), 0, 1 << 20) % (margin + 1)
    tallies = tallies.at[1:1 + 2 * couples:2].set(giver - moved).at[2:2 + 2 * couples:2].set(receiver + moved)
    return tallies[jax.random.permutation(jax.random.fold_in(rng, 2), count)]


def scatter_about(stream_key, shape, spread, limit, pieces=(), held_as=jnp.bfloat16):
    loudness = block_scale(stream_key, shape, pieces, -0.22, 0.18) if pieces else 1.0
    values = jax.random.normal(stream_key, shape, jnp.float32) * spread * loudness
    return jnp.minimum(jnp.maximum(values, -limit), limit).astype(held_as)


def setup_inputs(seed: int = 0) -> dict:
    keys = jax.random.split(jax.random.key(seed), 10)
    hidden = scatter_about(keys[0], (TOKENS, D), 1.0, 6.0, ((0, 32), (1, 4)))
    qkv_weight = scatter_about(keys[1], (LAYERS, D, 3, HD), D ** -0.5, 0.109375, ((0, 2), (3, 4)))
    qk_gain = jnp.clip(jnp.exp(math.log(2.0) - 0.43078295 * jax.random.uniform(keys[2], (LAYERS, 2, HEAD), jnp.float32) ** block_scale(keys[2], (LAYERS, 2, HEAD), ((0, 2),), -0.2, 0.2)), 1.3, 2.0)
    out_weight = scatter_about(keys[3], (LAYERS, HD, D), HD ** -0.5, 0.15625, ((0, 2), (1, 4)))
    mod_weight = scatter_about(keys[4], (LAYERS, TEMB, 6 * D), (TEMB // 4) ** -0.5, 0.5, ((0, 2), (2, 128)))
    stale_kv = draw_stale_kv(jax.random.fold_in(keys[9], 71), 0)
    patch_lengths = ragged_sizes(keys[6], NPATCH, TOKENS - TEXT, (TOKENS - TEXT) // 2, 2).astype(jnp.int32)
    positions = draw_positions(jax.random.fold_in(keys[9], 71), 0)
    timestep = jax.random.randint(keys[8], (1,), 0, 1000).astype(jnp.int32)
    return {"hidden": hidden, "qkv_weight": qkv_weight, "qk_gain": qk_gain, "out_weight": out_weight, "mod_weight": mod_weight, "stale_kv": stale_kv, "patch_lengths": patch_lengths, "positions": positions, "timestep": timestep}


def patch_index(index, bounds):
    video_row = index - TEXT
    patch_id = lax.optimization_barrier(jnp.sum((video_row[:, None] >= bounds[None, :-1]).astype(jnp.int32), axis=1))
    return jnp.where(index < TEXT, 0, patch_id).astype(jnp.int32)

def time_features(timestep):
    half_width = TEMB // 2
    frequency = jnp.exp(-math.log(10000.0) * jnp.arange(half_width).astype(jnp.float32) / half_width)
    phases = timestep.astype(jnp.float32)[:, None] * frequency[None, :]
    embedded = jnp.concatenate([jnp.cos(phases), jnp.sin(phases)], axis=1)
    return jax.nn.silu(embedded).astype(jnp.bfloat16)

def axis_freq(dim_size):
    return 1.0 / 10000.0 ** (jnp.arange(0, dim_size, 2).astype(jnp.float32) / dim_size)

def rope_tables(positions, head_count):
    coords = positions.astype(jnp.float32)
    angles = jnp.concatenate([coords[0][:, None] * axis_freq(HEAD // 4)[None, :], coords[1][:, None] * axis_freq(3 * HEAD // 8)[None, :], coords[2][:, None] * axis_freq(3 * HEAD // 8)[None, :]], axis=1)
    angles = jnp.repeat(angles, 2, axis=1)
    return (jnp.tile(jnp.cos(angles), (1, head_count)), jnp.tile(jnp.sin(angles), (1, head_count)))

def rotate_pairs(values):
    column = jnp.arange(values.shape[-1])
    return jnp.where(column % 2 == 0, -jnp.roll(values, -1, axis=-1), jnp.roll(values, 1, axis=-1))

def head_norm(values, gain):
    parts = values.reshape(values.shape[0], -1, HEAD)
    average = lax.optimization_barrier(jnp.mean(parts, axis=-1, keepdims=True))
    centred = parts - average
    variance = lax.optimization_barrier(jnp.mean(centred * centred, axis=-1, keepdims=True))
    return (centred * lax.rsqrt(variance + 1e-06) * gain).reshape(values.shape)

def layer_norm(values):
    average = lax.optimization_barrier(jnp.mean(values, axis=1, keepdims=True))
    centred = values - average
    variance = lax.optimization_barrier(jnp.mean(centred * centred, axis=1, keepdims=True))
    return centred * lax.rsqrt(variance + 1e-05)

def one_layer(incoming, w_qkv, gains, w_out, w_mod, stale, timestep, cosine, sine_table, video, patch_all):
    modulate = jnp.dot(time_features(timestep), w_mod, preferred_element_type=jnp.float32)[0].reshape(6, D)
    shift_rows = jnp.where(video, modulate[0], modulate[3])
    scale_rows = jnp.where(video, modulate[1], modulate[4])
    gate_rows = jnp.where(video, modulate[2], modulate[5])
    features_all = incoming.astype(jnp.float32)
    normed = (layer_norm(features_all) * (1.0 + scale_rows) + shift_rows).astype(jnp.bfloat16)
    proj = jnp.dot(normed, w_qkv.reshape(D, 3 * HD), preferred_element_type=jnp.float32).reshape(TOKENS, 3, HD)
    queries = head_norm(proj[:, 0], gains[0])
    key_vecs = head_norm(proj[:, 1], gains[1])
    queries = jnp.where(video, queries * cosine + rotate_pairs(queries) * sine_table, queries).astype(jnp.bfloat16)
    key_vecs = jnp.where(video, key_vecs * cosine + rotate_pairs(key_vecs) * sine_table, key_vecs).astype(jnp.bfloat16)
    values = proj[:, 2].astype(jnp.bfloat16)
    allowed = patch_all[None, :] <= patch_all[:, None]

    def heads_of(array):
        return array.reshape(TOKENS, HEADS, HEAD).transpose(1, 0, 2)

    def one_head(operands):
        query_h, fresh_k, fresh_v, stale_k, stale_v = [o.astype(jnp.float32) for o in operands]
        hi = lax.Precision.HIGHEST
        scores_fresh = jnp.dot(query_h, fresh_k.T, precision=hi)
        scores_stale = jnp.dot(query_h, stale_k.T, precision=hi)
        scores = jnp.where(allowed, scores_fresh, scores_stale) * HEAD ** (-0.5)
        highest = lax.optimization_barrier(jnp.max(scores, axis=1, keepdims=True))
        weights_soft = jnp.exp(scores - highest)
        denominator = lax.optimization_barrier(jnp.sum(weights_soft, axis=1, keepdims=True))
        part_fresh = lax.optimization_barrier(jnp.where(allowed, weights_soft, 0.0).astype(jnp.bfloat16)).astype(jnp.float32)
        part_stale = lax.optimization_barrier(jnp.where(allowed, 0.0, weights_soft).astype(jnp.bfloat16)).astype(jnp.float32)
        numer = jnp.dot(part_fresh, fresh_v, precision=hi) + jnp.dot(part_stale, stale_v, precision=hi)
        return (numer / denominator).astype(jnp.bfloat16)
    attended = lax.map(one_head, (heads_of(queries), heads_of(key_vecs), heads_of(values), heads_of(stale[0]), heads_of(stale[1])))
    attended = attended.transpose(1, 0, 2).reshape(TOKENS, HD)
    projected = jnp.dot(attended, w_out, preferred_element_type=jnp.float32)
    result = (features_all + gate_rows * projected).astype(jnp.bfloat16)
    return (result, jnp.stack([key_vecs, values]))

def reference(hidden, qkv_weight, qk_gain, out_weight, mod_weight, stale_kv, patch_lengths, positions, timestep):
    all_rows = jnp.arange(TOKENS).astype(jnp.int32)
    video = (all_rows >= TEXT)[:, None]
    bounds = jnp.cumsum(patch_lengths).astype(jnp.int32)
    patch_all = patch_index(all_rows, bounds)
    cosine, sine_table = rope_tables(positions, HEADS)
    outputs = []
    kv_list = []
    current = hidden
    for layer_idx in range(LAYERS):
        current, fresh = one_layer(current, qkv_weight[layer_idx], qk_gain[layer_idx], out_weight[layer_idx], mod_weight[layer_idx], stale_kv[layer_idx], timestep, cosine, sine_table, video, patch_all)
        outputs.append(current)
        kv_list.append(fresh)
    return (jnp.stack(outputs), jnp.stack(kv_list))
```

```python
import math

import jax
import jax.numpy as jnp
from jax import lax
from jax.sharding import PartitionSpec as P

HEAD = 64
TEMB = 512
TEXT = 226


def shifted(value, axis, steps):
    count = lax.axis_size(axis)
    first, last = (max(0, -steps), min(count, count - steps))
    return lax.ppermute(value, axis, [(source, source + steps) for source in range(first, last)])


def patch_index(index, bounds):
    video_row = index - TEXT
    patch_id = jnp.sum((video_row[:, None] >= bounds[None, :-1]).astype(jnp.int32), axis=1)
    return jnp.where(index < TEXT, 0, patch_id)


def time_features(timestep):
    half_width = TEMB // 2
    frequency = jnp.exp(
        -math.log(10000.0) * jnp.arange(half_width).astype(jnp.float32) / half_width
    )
    phases = timestep.astype(jnp.float32)[:, None] * frequency[None, :]
    embedded = jnp.concatenate([jnp.cos(phases), jnp.sin(phases)], axis=1)
    return jax.nn.silu(embedded).astype(jnp.bfloat16)


def axis_freq(dim_size):
    return 1.0 / 10000.0 ** (jnp.arange(0, dim_size, 2).astype(jnp.float32) / dim_size)


def rope_tables(positions, head_count):
    coords = positions.astype(jnp.float32)
    angles = jnp.concatenate(
        [
            coords[0][:, None] * axis_freq(HEAD // 4)[None, :],
            coords[1][:, None] * axis_freq(3 * HEAD // 8)[None, :],
            coords[2][:, None] * axis_freq(3 * HEAD // 8)[None, :],
        ],
        axis=1,
    )
    angles = jnp.repeat(angles, 2, axis=1)
    return (jnp.tile(jnp.cos(angles), (1, head_count)), jnp.tile(jnp.sin(angles), (1, head_count)))


def rotate_pairs(values):
    column = jnp.arange(values.shape[-1])
    return jnp.where(column % 2 == 0, -jnp.roll(values, -1, axis=-1), jnp.roll(values, 1, axis=-1))


def head_norm(values, gain):
    parts = values.reshape(values.shape[0], -1, HEAD)
    average = jnp.mean(parts, axis=-1, keepdims=True)
    centred = parts - average
    variance = jnp.mean(centred * centred, axis=-1, keepdims=True)
    return (centred * lax.rsqrt(variance + 1e-06) * gain).reshape(values.shape)


def merge_block(running, query_heads, query_patch, fresh_block, stale_block, bounds):
    highest, denominator, accumulated = running
    key_count = fresh_block.shape[1]
    head_count = query_heads.shape[1]
    key_rows = jnp.arange(key_count, dtype=jnp.int32)
    allowed = (patch_index(key_rows, bounds)[None, :] <= query_patch[:, None])[None]
    fresh_keys = fresh_block[0].reshape(key_count, head_count, HEAD)
    fresh_vals = fresh_block[1].reshape(key_count, head_count, HEAD)
    stale_keys = stale_block[0].reshape(key_count, head_count, HEAD)
    stale_vals = stale_block[1].reshape(key_count, head_count, HEAD)
    scores_fresh = jnp.einsum(
        "thd,rhd->htr", query_heads, fresh_keys, preferred_element_type=jnp.float32
    )
    scores_stale = jnp.einsum(
        "thd,rhd->htr", query_heads, stale_keys, preferred_element_type=jnp.float32
    )
    scores = jnp.where(allowed, scores_fresh, scores_stale) * HEAD ** (-0.5)
    new_high = jnp.maximum(highest, jnp.max(scores, axis=2))
    rescale = jnp.exp(highest - new_high)
    weights_soft = jnp.exp(scores - new_high[:, :, None])
    denominator = jnp.sum(weights_soft, axis=2)
    part_fresh = jnp.where(allowed, weights_soft, 0.0).astype(jnp.bfloat16)
    part_stale = jnp.where(allowed, 0.0, weights_soft).astype(jnp.bfloat16)
    accumulated = accumulated * rescale[:, :, None]
    accumulated = jnp.einsum(
        "htr,rhd->htd", part_fresh, fresh_vals, preferred_element_type=jnp.float32
    )
    accumulated = accumulated + jnp.einsum(
        "htr,rhd->htd", part_stale, stale_vals, preferred_element_type=jnp.float32
    )
    return (new_high, denominator, accumulated)


def local(
    hidden,
    qkv_weight,
    qk_gain,
    out_weight,
    mod_weight,
    stale_kv,
    patch_lengths,
    positions,
    timestep,
):
    tok_rows = hidden.shape[0]
    feat_share = hidden.shape[1]
    model_width = feat_share * lax.axis_size("tp")
    head_cols = qkv_weight.shape[3]
    head_count = head_cols // HEAD
    seq_rank = lax.axis_index("seq")
    tp_rank = lax.axis_index("tp")
    section_rank = lax.axis_index("section")
    mod_share = jnp.dot(time_features(timestep), mod_weight[0], preferred_element_type=jnp.float32)[
        0
    ]
    by_tp = lax.all_gather(mod_share[None, None, :], "tp", axis=0, tiled=True)
    modulate = lax.all_gather(
        jnp.pad(by_tp.reshape(1, 4, -1), ((0, 0), (0, 4), (0, 0))), "seq", axis=0, tiled=True
    )[:, :4].reshape(6, model_width)
    my_rows = seq_rank * tok_rows + jnp.arange(tok_rows, dtype=jnp.int32)
    video = (my_rows >= TEXT)[:, None]
    bounds = jnp.cumsum(patch_lengths)
    query_patch = patch_index(my_rows, bounds)
    cosine, sine_table = rope_tables(positions, head_count)
    shift_rows = jnp.where(video, modulate[0], modulate[3])
    scale_rows = jnp.where(video, modulate[1], modulate[4])
    gate_both = lax.dynamic_slice_in_dim(modulate, tp_rank * feat_share, feat_share, 1)
    gate_rows = jnp.where(video, gate_both[2], gate_both[5])
    weights_qkv = qkv_weight[0]
    gains = qk_gain[0]
    weights_out = out_weight[0]
    stale_own = stale_kv[0]

    def attend(queries, fresh_kv):
        query_heads = queries.reshape(tok_rows, head_count, HEAD)
        start_state = (
            jnp.full((head_count, tok_rows), -1e30, jnp.float32),
            jnp.zeros((head_count, tok_rows), jnp.float32),
            jnp.zeros((head_count, tok_rows, HEAD), jnp.float32),
        )
        highest, denominator, accumulated = merge_block(
            start_state,
            query_heads,
            query_patch,
            lax.all_gather(fresh_kv, "seq", axis=1, tiled=True),
            lax.all_gather(stale_own, "seq", axis=1, tiled=True),
            bounds,
        )
        blended = accumulated / denominator[:, :, None]
        return jnp.transpose(blended, (1, 0, 2)).reshape(tok_rows, head_cols).astype(jnp.bfloat16)

    def run_layer(incoming):
        features_all = lax.all_gather(incoming, "tp", axis=1, tiled=True).astype(jnp.float32)
        average = jnp.mean(features_all, axis=1, keepdims=True)
        centred = features_all - average
        variance = jnp.mean(centred * centred, axis=1, keepdims=True)
        normed = (centred * lax.rsqrt(variance + 1e-05) * (1.0 + scale_rows) + shift_rows).astype(
            jnp.bfloat16
        )
        proj = jnp.einsum("td,dcf->tcf", normed, weights_qkv, preferred_element_type=jnp.float32)
        queries = head_norm(proj[:, 0], gains[0])
        key_vecs = head_norm(proj[:, 1], gains[1])
        queries = jnp.where(
            video, queries * cosine + rotate_pairs(queries) * sine_table, queries
        ).astype(jnp.bfloat16)
        key_vecs = jnp.where(
            video, key_vecs * cosine + rotate_pairs(key_vecs) * sine_table, key_vecs
        ).astype(jnp.bfloat16)
        values = proj[:, 2].astype(jnp.bfloat16)
        fresh_kv = jnp.stack([key_vecs, values])
        attended = attend(queries, fresh_kv)
        projected = lax.psum_scatter(
            lax.dot_general(
                weights_out, attended, (((0,), (1,)), ((), ())), preferred_element_type=jnp.float32
            ).astype(jnp.bfloat16),
            "tp",
            scatter_dimension=0,
            tiled=True,
        ).astype(jnp.float32)
        result = (incoming.astype(jnp.float32) + gate_rows * projected.T).astype(jnp.bfloat16)
        return (result, fresh_kv)

    first_out, first_kv = run_layer(hidden)
    passed = shifted(first_out, "section", 1)
    second_out, second_kv = run_layer(passed)
    first_section = section_rank == 0
    hidden_out = jnp.where(first_section, first_out, second_out)[None]
    fresh_out = jnp.where(first_section, first_kv, second_kv)[None]
    return (hidden_out, fresh_out)


def solution(mesh):
    return jax.shard_map(
        local,
        mesh=mesh,
        in_specs=(
            P("seq", "tp"),
            P("section", None, None, "tp"),
            P("section", None, None),
            P("section", "tp", None),
            P("section", None, ("seq", "tp")),
            P("section", None, "seq", "tp"),
            P(),
            P(None, "seq"),
            P(),
        ),
        out_specs=(P("section", "seq", "tp"), P("section", None, "seq", "tp")),
        check_vma=False,
    )
```

```python
import math

import jax
import jax.numpy as jnp
from jax import lax
from jax.experimental import pallas as pl
from jax.experimental.pallas import tpu as pltpu
from jax.sharding import PartitionSpec as P

HEAD = 64
TEMB = 512
TEXT = 226


def patch_index(index, bounds):
    video_row = index - TEXT
    patch_id = jnp.sum((video_row[:, None] >= bounds[None, :-1]).astype(jnp.int32), axis=1)
    return jnp.where(index < TEXT, 0, patch_id)


def time_features(timestep):
    half_width = TEMB // 2
    frequency = jnp.exp(
        -math.log(10000.0) * jnp.arange(half_width).astype(jnp.float32) / half_width
    )
    phases = timestep.astype(jnp.float32)[:, None] * frequency[None, :]
    embedded = jnp.concatenate([jnp.cos(phases), jnp.sin(phases)], axis=1)
    return jax.nn.silu(embedded).astype(jnp.bfloat16)


def axis_freq(dim_size):
    return 1.0 / 10000.0 ** (jnp.arange(0, dim_size, 2).astype(jnp.float32) / dim_size)


def rope_tables(positions, head_count):
    coords = positions.astype(jnp.float32)
    angles = jnp.concatenate(
        [
            coords[0][:, None] * axis_freq(HEAD // 4)[None, :],
            coords[1][:, None] * axis_freq(3 * HEAD // 8)[None, :],
            coords[2][:, None] * axis_freq(3 * HEAD // 8)[None, :],
        ],
        axis=1,
    )
    angles = jnp.repeat(angles, 2, axis=1)
    return (jnp.tile(jnp.cos(angles), (1, head_count)), jnp.tile(jnp.sin(angles), (1, head_count)))


MESH = pl.DeviceIdType.MESH
OTHERS = (1, 3, 2)
VMEM_SPEC = pl.BlockSpec(memory_space=pltpu.VMEM)


def place():
    seq = lax.axis_index("seq")
    return seq // 8, (seq // 2) % 4, seq % 2


def seq_of(x, z, c):
    return (x * 4 + z) * 2 + c


def remote(source, target, send_sem, recv_sem, device):
    return pltpu.make_async_remote_copy(
        src_ref=source,
        dst_ref=target,
        send_sem=send_sem,
        recv_sem=recv_sem,
        device_id=device,
        device_id_type=MESH,
    )


def seq_peers():
    x, z, c = place()
    along_z = [{"seq": seq_of(x, (z + d) % 4, c)} for d in OTHERS]
    along_x = [{"seq": seq_of((x + d) % 4, z, c)} for d in OTHERS]
    return along_z + along_x + [{"seq": seq_of(x, z, 1 - c)}]


def tp_peers():
    tp = lax.axis_index("tp")
    return [{"tp": (tp + d) % 4} for d in OTHERS]


def greet(peers):
    barrier = pltpu.get_barrier_semaphore()
    for peer in peers:
        pl.semaphore_signal(barrier, inc=1, device_id=peer, device_id_type=MESH)
    pl.semaphore_wait(barrier, len(peers))


class SeqGather:
    def __init__(self, own, blocks, send_sems, recv_sems):
        self.own, self.blocks = own, blocks
        self.send_sems, self.recv_sems = send_sems, recv_sems

    def send(self, slot, source, x, z, c, device):
        remote(
            source,
            self.blocks.at[x, z, c],
            self.send_sems.at[slot],
            self.recv_sems.at[x, z, c],
            device,
        ).start()

    def arrived(self, x, z, c):
        block = self.blocks.at[x, z, c]
        remote(
            block, block, self.send_sems.at[0], self.recv_sems.at[x, z, c], seq_peers()[-1]
        ).wait_recv()

    def start(self):
        x, z, c = place()
        for k, peer in enumerate(seq_peers()):
            self.send(k, self.own, x, z, c, peer)

    def forward_z(self):
        x, z, c = place()
        peers = seq_peers()
        for i, d in enumerate(OTHERS):
            from_z = (z + d) % 4
            self.arrived(x, from_z, c)
            for k, peer in enumerate(peers[3:]):
                self.send(7 + 4 * i + k, self.blocks.at[x, from_z, c], x, from_z, c, peer)

    def forward_x(self):
        x, z, c = place()
        partner = seq_peers()[-1]
        for i, dz in enumerate((0,) + OTHERS):
            for k, dx in enumerate(OTHERS):
                from_x, from_z = (x + dx) % 4, (z + dz) % 4
                self.arrived(from_x, from_z, c)
                block = self.blocks.at[from_x, from_z, c]
                self.send(19 + 3 * i + k, block, from_x, from_z, c, partner)

    def finish(self):
        x, z, c = place()
        for dz in (0,) + OTHERS:
            for dx in (0,) + OTHERS:
                self.arrived((x + dx) % 4, (z + dz) % 4, 1 - c)

    def drain(self):
        x, z, c = place()
        block = self.blocks.at[x, z, c]
        for slot in range(GATHER_SENDS):
            remote(
                block, block, self.send_sems.at[slot], self.recv_sems.at[x, z, c], seq_peers()[-1]
            ).wait_send()


GATHER_SENDS = 7 + 12 + 12


def modulation_kernel(share_ref, out_ref, local_sem, tp_send, tp_recv, send_sems, recv_sems):
    x, z, c = place()
    tp = lax.axis_index("tp")
    greet(seq_peers() + tp_peers())
    own = out_ref.at[x, z, c]
    keep = pltpu.make_async_copy(share_ref, own.at[tp], local_sem)
    keep.start()
    copies = []
    for k, peer in enumerate(tp_peers()):
        copy = remote(share_ref, own.at[tp], tp_send.at[k], tp_recv.at[tp], peer)
        copy.start()
        copies.append(copy)
    keep.wait()
    for k, d in enumerate(OTHERS):
        source = (tp + d) % 4
        remote(
            share_ref, own.at[source], tp_send.at[k], tp_recv.at[source], tp_peers()[k]
        ).wait_recv()
    gather = SeqGather(own, out_ref, send_sems, recv_sems)
    gather.start()
    gather.forward_z()
    gather.forward_x()
    gather.finish()
    for copy in copies:
        copy.wait_send()
    gather.drain()


def gather_modulation(share):
    cols = share.shape[-1]
    return pl.pallas_call(
        modulation_kernel,
        out_shape=jax.ShapeDtypeStruct((4, 4, 2, 4, 1, cols), jnp.float32),
        in_specs=[VMEM_SPEC],
        out_specs=VMEM_SPEC,
        scratch_shapes=[
            pltpu.SemaphoreType.DMA,
            pltpu.SemaphoreType.DMA((3,)),
            pltpu.SemaphoreType.DMA((4,)),
            pltpu.SemaphoreType.DMA((GATHER_SENDS,)),
            pltpu.SemaphoreType.DMA((4, 4, 2)),
        ],
        compiler_params=pltpu.CompilerParams(collective_id=0, has_side_effects=True),
    )(share)


def head_norm_rope(values, gain, cosine, sine):
    lane = lax.broadcasted_iota(jnp.int32, (values.shape[0], 128), 1)
    low = lane < HEAD
    groups = []
    for g in range(values.shape[1] // 128):
        part = values[:, g * 128 : (g + 1) * 128]

        def average(t):
            first = jnp.sum(jnp.where(low, t, 0.0), axis=1, keepdims=True)
            second = jnp.sum(jnp.where(low, 0.0, t), axis=1, keepdims=True)
            return jnp.where(low, first, second) * (1.0 / HEAD)

        centred = part - average(part)
        unit = centred * lax.rsqrt(average(centred * centred) + 1e-06)
        unit = unit * gain[:, g * 128 : (g + 1) * 128]
        turned = jnp.where(lane % 2 == 0, pltpu.roll(unit, 127, 1), pltpu.roll(unit, 1, 1))
        cos_part = cosine[:, g * 128 : (g + 1) * 128]
        groups.append(unit * cos_part + turned * sine[:, g * 128 : (g + 1) * 128])
    return jnp.concatenate(groups, axis=1)


def layer_kernel(
    hidden_ref,
    w_qkv_hbm,
    w_out_hbm,
    stale_ref,
    mod_ref,
    gain_ref,
    cos_ref,
    sin_ref,
    video_ref,
    limit_ref,
    out_ref,
    kv_ref,
    w_qkv,
    w_out,
    x_all,
    stale_all,
    fresh_all,
    partial,
    reduced,
    w_sems,
    x_send,
    x_recv,
    pass_send,
    r_send,
    r_recv,
    stale_send,
    stale_recv,
    fresh_send,
    fresh_recv,
):
    x, z, c = place()
    tp = lax.axis_index("tp")
    section = lax.axis_index("section")
    rows, share = hidden_ref.shape
    head_cols = w_qkv.shape[2]
    heads = head_cols // HEAD
    load_qkv = pltpu.make_async_copy(w_qkv_hbm, w_qkv, w_sems.at[0])
    load_out = pltpu.make_async_copy(w_out_hbm, w_out, w_sems.at[1])
    load_qkv.start()
    load_out.start()
    across = [{"section": 1 - section, "tp": (tp + d) % 4} for d in (0,) + OTHERS]
    greet(tp_peers() + seq_peers() + across)

    @pl.when(section == 0)
    def _():
        for k, peer in enumerate(tp_peers()):
            remote(hidden_ref, x_all.at[tp], x_send.at[k], x_recv.at[tp], peer).start()
        x_all[tp] = hidden_ref[...]

    stale = SeqGather(stale_ref, stale_all, stale_send, stale_recv)
    stale.start()
    stale_all[x, z, c] = stale_ref[...]

    def x_arrived(source):
        remote(
            hidden_ref, x_all.at[source], x_send.at[0], x_recv.at[source], tp_peers()[0]
        ).wait_recv()

    @pl.when(section == 1)
    def _():
        stale.forward_z()
        stale.forward_x()
        stale.finish()
        x_arrived(tp)

    for d in OTHERS:
        x_arrived((tp + d) % 4)

    video = video_ref[...] > 0.0
    width = share * 4
    total = jnp.zeros((rows, 1), jnp.float32)
    for t in range(4):
        total += jnp.sum(x_all[t].astype(jnp.float32), axis=1, keepdims=True)
    mean = total * (1.0 / width)
    square = jnp.zeros((rows, 1), jnp.float32)
    for t in range(4):
        centred = x_all[t].astype(jnp.float32) - mean
        square += jnp.sum(centred * centred, axis=1, keepdims=True)
    inverse = lax.rsqrt(square * (1.0 / width) + 1e-05)

    @pl.when(section == 0)
    def _():
        stale.forward_z()

    load_qkv.wait()
    proj = [jnp.zeros((rows, head_cols), jnp.float32) for _ in range(3)]
    for t in range(4):
        cols = slice(t * share, (t + 1) * share)
        shift = jnp.where(video, mod_ref[0:1, cols], mod_ref[3:4, cols])
        scale = jnp.where(video, mod_ref[1:2, cols], mod_ref[4:5, cols])
        centred = x_all[t].astype(jnp.float32) - mean
        normed = (centred * inverse * (1.0 + scale) + shift).astype(jnp.bfloat16)
        for part in (1, 2, 0):
            proj[part] += jnp.dot(normed, w_qkv[part, cols, :], preferred_element_type=jnp.float32)
    cosine, sine = cos_ref[...], sin_ref[...]
    keys = head_norm_rope(proj[1], gain_ref[1:2, :], cosine, sine).astype(jnp.bfloat16)
    kv_ref[0] = keys
    kv_ref[1] = proj[2].astype(jnp.bfloat16)
    fresh_all[x, z, c, 0] = keys
    fresh_all[x, z, c, 1] = proj[2].astype(jnp.bfloat16)
    fresh = SeqGather(kv_ref, fresh_all, fresh_send, fresh_recv)
    fresh.start()

    @pl.when(section == 0)
    def _():
        stale.forward_x()

    queries = head_norm_rope(proj[0], gain_ref[0:1, :], cosine, sine)
    stacked = jnp.concatenate([queries] * heads, axis=0)
    row_head = lax.broadcasted_iota(jnp.int32, stacked.shape, 0) // rows
    col_head = lax.broadcasted_iota(jnp.int32, stacked.shape, 1) // HEAD
    spread = jnp.where(row_head == col_head, stacked, 0.0).astype(jnp.bfloat16)
    fresh.forward_z()

    @pl.when(section == 0)
    def _():
        stale.finish()

    tokens = rows * 32

    def all_rows(blocks, which):
        return blocks[:, :, :, which].reshape(tokens, head_cols)

    contract = (((1,), (1,)), ((), ()))
    scores_stale = lax.dot_general(
        spread, all_rows(stale_all, 0), contract, preferred_element_type=jnp.float32
    )
    fresh.forward_x()
    fresh.finish()
    scores_fresh = lax.dot_general(
        spread, all_rows(fresh_all, 0), contract, preferred_element_type=jnp.float32
    )
    column = lax.broadcasted_iota(jnp.int32, scores_fresh.shape, 1)
    allowed = column < limit_ref[...]
    scores = jnp.where(allowed, scores_fresh, scores_stale) * HEAD ** (-0.5)
    weights = jnp.exp(scores - jnp.max(scores, axis=1, keepdims=True))
    denominator = jnp.sum(weights, axis=1, keepdims=True)
    part_fresh = jnp.where(allowed, weights, 0.0).astype(jnp.bfloat16)
    part_stale = jnp.where(allowed, 0.0, weights).astype(jnp.bfloat16)
    mixed = jnp.dot(part_fresh, all_rows(fresh_all, 1), preferred_element_type=jnp.float32)
    mixed += jnp.dot(part_stale, all_rows(stale_all, 1), preferred_element_type=jnp.float32)
    mixed = jnp.where(row_head == col_head, mixed / denominator, 0.0)
    attended = mixed[0:rows]
    for h in range(1, heads):
        attended += mixed[h * rows : (h + 1) * rows]
    attended = attended.astype(jnp.bfloat16)

    load_out.wait()
    for t in range(4):
        partial[t] = jnp.dot(
            attended, w_out[:, t * share : (t + 1) * share], preferred_element_type=jnp.float32
        ).astype(jnp.bfloat16)
    r_copies = []
    for k, d in enumerate(OTHERS):
        target = (tp + d) % 4
        copy = remote(
            partial.at[target], reduced.at[tp], r_send.at[k], r_recv.at[tp], {"tp": target}
        )
        copy.start()
        r_copies.append(copy)
    mine = pl.ds(pl.multiple_of(tp * share, 128), share)
    gate = jnp.where(video, mod_ref[2:3, mine], mod_ref[5:6, mine])
    projected = partial[tp].astype(jnp.float32)
    for k, d in enumerate(OTHERS):
        source = (tp + d) % 4
        remote(
            partial.at[source], reduced.at[source], r_send.at[k], r_recv.at[source], {"tp": source}
        ).wait_recv()
        projected += reduced[source].astype(jnp.float32)
    out_ref[...] = (x_all[tp].astype(jnp.float32) + gate * projected).astype(jnp.bfloat16)

    @pl.when(section == 0)
    def _():
        passes = []
        for k, peer in enumerate(across):
            copy = remote(out_ref, x_all.at[tp], pass_send.at[k], x_recv.at[tp], peer)
            copy.start()
            passes.append(copy)
        for k, peer in enumerate(tp_peers()):
            remote(hidden_ref, x_all.at[tp], x_send.at[k], x_recv.at[tp], peer).wait_send()
        for copy in passes:
            copy.wait_send()

    for copy in r_copies:
        copy.wait_send()
    stale.drain()
    fresh.drain()


def run_layers(hidden, w_qkv, w_out, stale, modulate, gains, cosine, sine, video, limits):
    rows, share = hidden.shape
    head_cols = w_out.shape[0]
    blocks = pltpu.VMEM((4, 4, 2, 2, rows, head_cols), jnp.bfloat16)
    dma = pltpu.SemaphoreType.DMA
    any_spec = pl.BlockSpec(memory_space=pl.ANY)
    return pl.pallas_call(
        layer_kernel,
        out_shape=(
            jax.ShapeDtypeStruct((rows, share), jnp.bfloat16),
            jax.ShapeDtypeStruct((2, rows, head_cols), jnp.bfloat16),
        ),
        in_specs=[VMEM_SPEC, any_spec, any_spec] + [VMEM_SPEC] * 7,
        out_specs=(VMEM_SPEC, VMEM_SPEC),
        scratch_shapes=[
            pltpu.VMEM(w_qkv.shape, jnp.bfloat16),
            pltpu.VMEM(w_out.shape, jnp.bfloat16),
            pltpu.VMEM((4, rows, share), jnp.bfloat16),
            blocks,
            blocks,
            pltpu.VMEM((4, rows, share), jnp.bfloat16),
            pltpu.VMEM((4, rows, share), jnp.bfloat16),
            dma((2,)),
            dma((3,)),
            dma((4,)),
            dma((4,)),
            dma((3,)),
            dma((4,)),
            dma((GATHER_SENDS,)),
            dma((4, 4, 2)),
            dma((GATHER_SENDS,)),
            dma((4, 4, 2)),
        ],
        compiler_params=pltpu.CompilerParams(collective_id=1, has_side_effects=True),
    )(hidden, w_qkv, w_out, stale, modulate, gains, cosine, sine, video, limits)


def local(
    hidden,
    qkv_weight,
    qk_gain,
    out_weight,
    mod_weight,
    stale_kv,
    patch_lengths,
    positions,
    timestep,
):
    tok_rows = hidden.shape[0]
    head_count = qkv_weight.shape[3] // HEAD
    seq_rank = lax.axis_index("seq")
    share = jnp.dot(time_features(timestep), mod_weight[0], preferred_element_type=jnp.float32)
    modulate = gather_modulation(share).reshape(6, -1)
    my_rows = seq_rank * tok_rows + jnp.arange(tok_rows, dtype=jnp.int32)
    video = (my_rows >= TEXT)[:, None]
    bounds = jnp.cumsum(patch_lengths)
    query_patch = patch_index(my_rows, bounds)
    ends = jnp.where(jnp.arange(bounds.shape[0]) == bounds.shape[0] - 1, 1 << 30, TEXT + bounds)
    is_patch = query_patch[:, None] == jnp.arange(bounds.shape[0])[None, :]
    limits = jnp.sum(jnp.where(is_patch, ends[None, :], 0), axis=1, keepdims=True)
    limits = jnp.tile(limits.astype(jnp.int32), (head_count, 1))
    cosine, sine = rope_tables(positions, head_count)
    even = jnp.arange(cosine.shape[1]) % 2 == 0
    cosine = jnp.where(video, cosine, 1.0)
    sine = jnp.where(video, jnp.where(even, -sine, sine), 0.0)
    result, fresh_kv = run_layers(
        hidden,
        jnp.transpose(qkv_weight[0], (1, 0, 2)),
        out_weight[0],
        stale_kv[0],
        modulate,
        jnp.tile(qk_gain[0], (1, head_count)),
        cosine,
        sine,
        video.astype(jnp.float32),
        limits,
    )
    return (result[None], fresh_kv[None])


def solution(mesh):
    return jax.shard_map(
        local,
        mesh=mesh,
        in_specs=(
            P("seq", "tp"),
            P("section", None, None, "tp"),
            P("section", None, None),
            P("section", "tp", None),
            P("section", None, ("seq", "tp")),
            P("section", None, "seq", "tp"),
            P(),
            P(None, "seq"),
            P(),
        ),
        out_specs=(P("section", "seq", "tp"), P("section", None, "seq", "tp")),
        check_vma=False,
    )
```

```python
import math

import jax
import jax.numpy as jnp
from jax import lax
from jax.experimental import pallas as pl
from jax.experimental.pallas import tpu as pltpu
from jax.sharding import PartitionSpec as P

HEAD = 64
TEMB = 512
TEXT = 226


def time_features(timestep):
    half_width = TEMB // 2
    frequency = jnp.exp(
        -math.log(10000.0) * jnp.arange(half_width).astype(jnp.float32) / half_width
    )
    phases = timestep.astype(jnp.float32)[:, None] * frequency[None, :]
    embedded = jnp.concatenate([jnp.cos(phases), jnp.sin(phases)], axis=1)
    return jax.nn.silu(embedded).astype(jnp.bfloat16)


MESH = pl.DeviceIdType.MESH
OTHERS = (1, 3, 2)
VMEM_SPEC = pl.BlockSpec(memory_space=pltpu.VMEM)


def place():
    seq = lax.axis_index("seq")
    return seq // 8, (seq // 2) % 4, seq % 2


def seq_of(x, z, c):
    return (x * 4 + z) * 2 + c


def remote(source, target, send_sem, recv_sem, device):
    return pltpu.make_async_remote_copy(
        src_ref=source,
        dst_ref=target,
        send_sem=send_sem,
        recv_sem=recv_sem,
        device_id=device,
        device_id_type=MESH,
    )


def seq_peers():
    x, z, c = place()
    along_z = [{"seq": seq_of(x, (z + d) % 4, c)} for d in OTHERS]
    along_x = [{"seq": seq_of((x + d) % 4, z, c)} for d in OTHERS]
    return along_z + along_x + [{"seq": seq_of(x, z, 1 - c)}]


def tp_peers():
    tp = lax.axis_index("tp")
    return [{"tp": (tp + d) % 4} for d in OTHERS]


def greet(peers):
    barrier = pltpu.get_barrier_semaphore()
    for peer in peers:
        pl.semaphore_signal(barrier, inc=1, device_id=peer, device_id_type=MESH)
    pl.semaphore_wait(barrier, len(peers))


class SeqGather:
    def __init__(self, own, blocks, send_sems, recv_sems):
        self.own, self.blocks = own, blocks
        self.send_sems, self.recv_sems = send_sems, recv_sems

    def send(self, slot, source, x, z, c, device):
        remote(
            source,
            self.blocks.at[x, z, c],
            self.send_sems.at[slot],
            self.recv_sems.at[x, z, c],
            device,
        ).start()

    def arrived(self, x, z, c):
        block = self.blocks.at[x, z, c]
        remote(
            block, block, self.send_sems.at[0], self.recv_sems.at[x, z, c], seq_peers()[-1]
        ).wait_recv()

    def start_z(self):
        x, z, c = place()
        for k, peer in enumerate(seq_peers()[:3]):
            self.send(k, self.own, x, z, c, peer)

    def start_x(self):
        x, z, c = place()
        for k, peer in enumerate(seq_peers()[3:]):
            self.send(3 + k, self.own, x, z, c, peer)

    def start(self):
        self.start_z()
        self.start_x()

    def forward_z(self):
        x, z, c = place()
        peers = seq_peers()
        for i, d in enumerate(OTHERS):
            from_z = (z + d) % 4
            self.arrived(x, from_z, c)
            for k, peer in enumerate(peers[3:]):
                self.send(7 + 4 * i + k, self.blocks.at[x, from_z, c], x, from_z, c, peer)

    def forward_x(self):
        x, z, c = place()
        partner = seq_peers()[-1]
        for i, dz in enumerate((0,) + OTHERS):
            for k, dx in enumerate(OTHERS):
                from_x, from_z = (x + dx) % 4, (z + dz) % 4
                self.arrived(from_x, from_z, c)
                block = self.blocks.at[from_x, from_z, c]
                self.send(19 + 3 * i + k, block, from_x, from_z, c, partner)

    def finish(self):
        x, z, c = place()
        for dz in (0,) + OTHERS:
            for dx in (0,) + OTHERS:
                self.arrived((x + dx) % 4, (z + dz) % 4, 1 - c)

    def drain(self):
        x, z, c = place()
        block = self.blocks.at[x, z, c]
        for slot in range(GATHER_SENDS):
            remote(
                block, block, self.send_sems.at[slot], self.recv_sems.at[x, z, c], seq_peers()[-1]
            ).wait_send()


GATHER_SENDS = 7 + 12 + 12


def head_norm_rope(values, gain, cosine, sine):
    lane = lax.broadcasted_iota(jnp.int32, (values.shape[0], 128), 1)
    low = lane < HEAD
    groups = []
    for g in range(values.shape[1] // 128):
        part = values[:, g * 128 : (g + 1) * 128]

        def average(t):
            first = jnp.sum(jnp.where(low, t, 0.0), axis=1, keepdims=True)
            second = jnp.sum(jnp.where(low, 0.0, t), axis=1, keepdims=True)
            return jnp.where(low, first, second) * (1.0 / HEAD)

        centred = part - average(part)
        unit = centred * lax.rsqrt(average(centred * centred) + 1e-06)
        unit = unit * gain
        turned = jnp.where(lane % 2 == 0, pltpu.roll(unit, 127, 1), pltpu.roll(unit, 1, 1))
        groups.append(unit * cosine + turned * sine)
    return jnp.concatenate(groups, axis=1)


def layer_kernel(
    hidden_ref,
    w_qkv_hbm,
    w_out_hbm,
    stale_ref,
    mod_ref,
    gain_ref,
    cos_ref,
    sin_ref,
    length_ref,
    out_ref,
    kv_ref,
    w_qkv,
    w_out,
    x_all,
    stale_all,
    fresh_all,
    partial,
    reduced,
    mod_all,
    mod_tiles,
    w_sems,
    x_send,
    x_recv,
    pass_send,
    r_send,
    r_recv,
    stale_send,
    stale_recv,
    fresh_send,
    fresh_recv,
    mod_local,
    mod_tp_send,
    mod_tp_recv,
    mod_send,
    mod_recv,
):
    x, z, c = place()
    tp = lax.axis_index("tp")
    section = lax.axis_index("section")
    rows, share = hidden_ref.shape
    head_cols = w_qkv.shape[2]
    heads = head_cols // HEAD
    load_qkv = pltpu.make_async_copy(w_qkv_hbm, w_qkv, w_sems.at[0])
    load_out = pltpu.make_async_copy(w_out_hbm, w_out, w_sems.at[1])
    load_qkv.start()
    load_out.start()
    across = [{"section": 1 - section, "tp": (tp + d) % 4} for d in (0,) + OTHERS]
    greet(tp_peers() + seq_peers() + across)

    own_mod = mod_all.at[x, z, c]
    keep = pltpu.make_async_copy(mod_ref, own_mod.at[tp], mod_local)
    keep.start()

    def mod_copy(k, source):
        return remote(
            mod_ref, own_mod.at[source], mod_tp_send.at[k], mod_tp_recv.at[source], tp_peers()[k]
        )

    for k in range(3):
        mod_copy(k, tp).start()

    @pl.when(section == 0)
    def _():
        for k, peer in enumerate(tp_peers()):
            remote(hidden_ref, x_all.at[tp], x_send.at[k], x_recv.at[tp], peer).start()
        x_all[tp] = hidden_ref[...]

    keep.wait()
    for k, d in enumerate(OTHERS):
        mod_copy(k, (tp + d) % 4).wait_recv()
    stale = SeqGather(stale_ref, stale_all, stale_send, stale_recv)
    modulation = SeqGather(own_mod, mod_all, mod_send, mod_recv)
    modulation.start()
    stale.start_z()
    stale_all[x, z, c] = stale_ref[...]
    modulation.forward_z()
    stale.start_x()

    def x_arrived(source):
        remote(
            hidden_ref, x_all.at[source], x_send.at[0], x_recv.at[source], tp_peers()[0]
        ).wait_recv()

    modulation.forward_x()
    modulation.finish()
    groups = mod_all[...].reshape(16, 8, 2, 128)
    blank = jnp.zeros((16, 1, 128), jnp.float32)
    mod_tiles[...] = jnp.concatenate([groups[:, :, 0], blank], axis=1) + jnp.concatenate(
        [blank, groups[:, :, 1]], axis=1
    )
    stale.forward_z()

    @pl.when(section == 1)
    def _():
        stale.forward_x()
        stale.finish()
        x_arrived(tp)

    for d in OTHERS:
        x_arrived((tp + d) % 4)

    token = lax.axis_index("seq") * rows + lax.broadcasted_iota(jnp.int32, (rows, 1), 0)
    video = token >= TEXT
    width = share * 4
    tiles = share // 128

    def mod_tile(row, index):
        tile = row * (width // 128) + index
        return mod_tiles[tile // 9, tile % 9 : tile % 9 + 1, :]

    def mod_rows(row, t):
        parts = [
            jnp.where(video, mod_tile(row, t * tiles + i), mod_tile(row + 3, t * tiles + i))
            for i in range(tiles)
        ]
        return jnp.concatenate(parts, axis=1)

    total = jnp.zeros((rows, 1), jnp.float32)
    for t in range(4):
        total += jnp.sum(x_all[t].astype(jnp.float32), axis=1, keepdims=True)
    mean = total * (1.0 / width)
    square = jnp.zeros((rows, 1), jnp.float32)
    for t in range(4):
        centred = x_all[t].astype(jnp.float32) - mean
        square += jnp.sum(centred * centred, axis=1, keepdims=True)
    inverse = lax.rsqrt(square * (1.0 / width) + 1e-05)
    load_qkv.wait()
    proj = [jnp.zeros((rows, head_cols), jnp.float32) for _ in range(3)]
    for t in range(4):
        cols = slice(t * share, (t + 1) * share)
        shift = mod_rows(0, t)
        scale = mod_rows(1, t)
        centred = x_all[t].astype(jnp.float32) - mean
        normed = (centred * inverse * (1.0 + scale) + shift).astype(jnp.bfloat16)
        for part in (1, 2, 0):
            proj[part] += jnp.dot(normed, w_qkv[part, cols, :], preferred_element_type=jnp.float32)
    cosine, sine = cos_ref[...], sin_ref[...]
    gains = jnp.concatenate([gain_ref[...]] * 2, axis=1)
    keys = head_norm_rope(proj[1], gains[1:2], cosine, sine).astype(jnp.bfloat16)
    kv_ref[0] = keys
    kv_ref[1] = proj[2].astype(jnp.bfloat16)
    fresh_all[x, z, c, 0] = keys
    fresh_all[x, z, c, 1] = proj[2].astype(jnp.bfloat16)
    fresh = SeqGather(kv_ref, fresh_all, fresh_send, fresh_recv)
    fresh.start()

    @pl.when(section == 0)
    def _():
        stale.forward_x()

    queries = head_norm_rope(proj[0], gains[0:1], cosine, sine)
    stacked = jnp.concatenate([queries] * heads, axis=0)
    row_head = lax.broadcasted_iota(jnp.int32, stacked.shape, 0) // rows
    col_head = lax.broadcasted_iota(jnp.int32, stacked.shape, 1) // HEAD
    spread = jnp.where(row_head == col_head, stacked, 0.0).astype(jnp.bfloat16)
    fresh.forward_z()

    @pl.when(section == 0)
    def _():
        stale.finish()

    tokens = rows * 32

    def all_rows(blocks, which):
        return blocks[:, :, :, which].reshape(tokens, head_cols)

    contract = (((1,), (1,)), ((), ()))
    scores_stale = lax.dot_general(
        spread, all_rows(stale_all, 0), contract, preferred_element_type=jnp.float32
    )
    fresh.forward_x()
    fresh.finish()
    scores_fresh = lax.dot_general(
        spread, all_rows(fresh_all, 0), contract, preferred_element_type=jnp.float32
    )
    column = lax.broadcasted_iota(jnp.int32, scores_fresh.shape, 1)
    first = TEXT + length_ref[0]
    second = first + length_ref[1]
    third = second + length_ref[2]
    limit = jnp.where(token < third, third, tokens)
    limit = jnp.where(token < first, first, jnp.where(token < second, second, limit))
    allowed = column < jnp.concatenate([limit] * heads, axis=0)
    scores = jnp.where(allowed, scores_fresh, scores_stale) * HEAD ** (-0.5)
    weights = jnp.exp(scores - jnp.max(scores, axis=1, keepdims=True))
    denominator = jnp.sum(weights, axis=1, keepdims=True)
    part_fresh = jnp.where(allowed, weights, 0.0).astype(jnp.bfloat16)
    part_stale = jnp.where(allowed, 0.0, weights).astype(jnp.bfloat16)
    mixed = jnp.dot(part_fresh, all_rows(fresh_all, 1), preferred_element_type=jnp.float32)
    mixed += jnp.dot(part_stale, all_rows(stale_all, 1), preferred_element_type=jnp.float32)
    mixed = jnp.where(row_head == col_head, mixed / denominator, 0.0)
    attended = mixed[0:rows]
    for h in range(1, heads):
        attended += mixed[h * rows : (h + 1) * rows]
    attended = attended.astype(jnp.bfloat16)

    load_out.wait()
    for t in range(4):
        partial[t] = jnp.dot(
            attended, w_out[:, t * share : (t + 1) * share], preferred_element_type=jnp.float32
        ).astype(jnp.bfloat16)
    r_copies = []
    for k, d in enumerate(OTHERS):
        target = (tp + d) % 4
        copy = remote(
            partial.at[target], reduced.at[tp], r_send.at[k], r_recv.at[tp], {"tp": target}
        )
        copy.start()
        r_copies.append(copy)
    gate = jnp.zeros((rows, share), jnp.float32)
    for t in range(4):
        gate = jnp.where(tp == t, mod_rows(2, t), gate)
    projected = partial[tp].astype(jnp.float32)
    for k, d in enumerate(OTHERS):
        source = (tp + d) % 4
        remote(
            partial.at[source], reduced.at[source], r_send.at[k], r_recv.at[source], {"tp": source}
        ).wait_recv()
        projected += reduced[source].astype(jnp.float32)
    out_ref[...] = (x_all[tp].astype(jnp.float32) + gate * projected).astype(jnp.bfloat16)

    @pl.when(section == 0)
    def _():
        passes = []
        for k, peer in enumerate(across):
            copy = remote(out_ref, x_all.at[tp], pass_send.at[k], x_recv.at[tp], peer)
            copy.start()
            passes.append(copy)
        for k, peer in enumerate(tp_peers()):
            remote(hidden_ref, x_all.at[tp], x_send.at[k], x_recv.at[tp], peer).wait_send()
        for copy in passes:
            copy.wait_send()

    for copy in r_copies:
        copy.wait_send()
    for k in range(3):
        mod_copy(k, tp).wait_send()
    modulation.drain()
    stale.drain()
    fresh.drain()


def run_layers(hidden, w_qkv, w_out, stale, modulate, gains, cosine, sine, lengths):
    rows, share = hidden.shape
    head_cols = w_out.shape[0]
    blocks = pltpu.VMEM((4, 4, 2, 2, rows, head_cols), jnp.bfloat16)
    dma = pltpu.SemaphoreType.DMA
    any_spec = pl.BlockSpec(memory_space=pl.ANY)
    return pl.pallas_call(
        layer_kernel,
        out_shape=(
            jax.ShapeDtypeStruct((rows, share), jnp.bfloat16),
            jax.ShapeDtypeStruct((2, rows, head_cols), jnp.bfloat16),
        ),
        in_specs=[VMEM_SPEC, any_spec, any_spec]
        + [VMEM_SPEC] * 5
        + [pl.BlockSpec(memory_space=pltpu.SMEM)],
        out_specs=(VMEM_SPEC, VMEM_SPEC),
        scratch_shapes=[
            pltpu.VMEM(w_qkv.shape, jnp.bfloat16),
            pltpu.VMEM(w_out.shape, jnp.bfloat16),
            pltpu.VMEM((4, rows, share), jnp.bfloat16),
            blocks,
            blocks,
            pltpu.VMEM((4, rows, share), jnp.bfloat16),
            pltpu.VMEM((4, rows, share), jnp.bfloat16),
            pltpu.VMEM((4, 4, 2, 4, 2, 128), jnp.float32),
            pltpu.VMEM((16, 9, 128), jnp.float32),
            dma((2,)),
            dma((3,)),
            dma((4,)),
            dma((4,)),
            dma((3,)),
            dma((4,)),
            dma((GATHER_SENDS,)),
            dma((4, 4, 2)),
            dma((GATHER_SENDS,)),
            dma((4, 4, 2)),
            dma,
            dma((3,)),
            dma((4,)),
            dma((GATHER_SENDS,)),
            dma((4, 4, 2)),
        ],
        compiler_params=pltpu.CompilerParams(collective_id=0, has_side_effects=True),
    )(hidden, w_qkv, w_out, stale, modulate, gains, cosine, sine, lengths)


def rope_tables(positions, first_row):
    column = jnp.arange(128)
    pair = (column % HEAD) // 2
    spans = ((0, HEAD // 4), (HEAD // 8, 3 * HEAD // 8), (5 * HEAD // 16, 3 * HEAD // 8))
    coords = positions.astype(jnp.float32)
    angles = jnp.zeros((positions.shape[1], 128), jnp.float32)
    for axis, (start, size) in enumerate(spans):
        exponent = 2.0 * (pair - start).astype(jnp.float32) / size
        inside = (pair >= start) & (pair < start + size // 2)
        frequency = jnp.where(inside, 1.0 / 10000.0**exponent, 0.0)
        angles = angles + coords[axis][:, None] * frequency[None, :]
    video = (first_row + jnp.arange(positions.shape[1]) >= TEXT)[:, None]
    sign = jnp.where(column % 2 == 0, -1.0, 1.0)[None, :]
    cosine = jnp.where(video, jnp.cos(angles), 1.0)
    return cosine, jnp.where(video, jnp.sin(angles) * sign, 0.0)


def local(
    hidden,
    qkv_weight,
    qk_gain,
    out_weight,
    mod_weight,
    stale_kv,
    patch_lengths,
    positions,
    timestep,
):
    tok_rows = hidden.shape[0]
    seq_rank = lax.axis_index("seq")
    share = jnp.dot(time_features(timestep), mod_weight[0], preferred_element_type=jnp.float32)
    device = seq_rank * lax.axis_size("tp") + lax.axis_index("tp")
    offset = (share.shape[1] * device) % 128
    placed = lax.dynamic_update_slice(jnp.zeros((1, 256), jnp.float32), share, (0, offset))
    cosine, sine = rope_tables(positions, seq_rank * tok_rows)
    result, fresh_kv = run_layers(
        hidden,
        jnp.transpose(qkv_weight[0], (1, 0, 2)),
        out_weight[0],
        stale_kv[0],
        placed.reshape(2, 128),
        qk_gain[0],
        cosine,
        sine,
        patch_lengths,
    )
    return (result[None], fresh_kv[None])


def solution(mesh):
    return jax.shard_map(
        local,
        mesh=mesh,
        in_specs=(
            P("seq", "tp"),
            P("section", None, None, "tp"),
            P("section", None, None),
            P("section", "tp", None),
            P("section", None, ("seq", "tp")),
            P("section", None, "seq", "tp"),
            P(),
            P(None, "seq"),
            P(),
        ),
        out_specs=(P("section", "seq", "tp"), P("section", None, "seq", "tp")),
        check_vma=False,
    )
```

```python
import math

import jax
import jax.numpy as jnp
from jax import lax
from jax.experimental import pallas as pl
from jax.experimental.pallas import tpu as pltpu
from jax.sharding import PartitionSpec as P

HEAD = 64
TEMB = 512
TEXT = 226


def time_features(timestep):
    half_width = TEMB // 2
    frequency = jnp.exp(
        -math.log(10000.0) * jnp.arange(half_width).astype(jnp.float32) / half_width
    )
    phases = timestep.astype(jnp.float32)[:, None] * frequency[None, :]
    embedded = jnp.concatenate([jnp.cos(phases), jnp.sin(phases)], axis=1)
    return jax.nn.silu(embedded).astype(jnp.bfloat16)


MESH = pl.DeviceIdType.MESH
OTHERS = (1, 3, 2)
VMEM_SPEC = pl.BlockSpec(memory_space=pltpu.VMEM)


def place():
    seq = lax.axis_index("seq")
    return seq // 8, (seq // 2) % 4, seq % 2


def seq_of(x, z, c):
    return (x * 4 + z) * 2 + c


def remote(source, target, send_sem, recv_sem, device):
    return pltpu.make_async_remote_copy(
        src_ref=source,
        dst_ref=target,
        send_sem=send_sem,
        recv_sem=recv_sem,
        device_id=device,
        device_id_type=MESH,
    )


def seq_peers():
    x, z, c = place()
    along_z = [{"seq": seq_of(x, (z + d) % 4, c)} for d in OTHERS]
    along_x = [{"seq": seq_of((x + d) % 4, z, c)} for d in OTHERS]
    return along_z + along_x + [{"seq": seq_of(x, z, 1 - c)}]


def tp_peers():
    tp = lax.axis_index("tp")
    return [{"tp": (tp + d) % 4} for d in OTHERS]


def chip_column_peers():
    x, z, c = place()
    pairs = [(dz, dc) for dz in (0,) + OTHERS for dc in (0, 1) if (dz, dc) != (0, 0)]
    return [{"seq": seq_of(x, (z + dz) % 4, (c + dc) % 2)} for dz, dc in pairs]


def plane_peers():
    x, z, c = place()
    tp = lax.axis_index("tp")
    pairs = [(dx, dt) for dx in (0,) + OTHERS for dt in (0,) + OTHERS if (dx, dt) != (0, 0)]
    return [{"seq": seq_of((x + dx) % 4, z, c), "tp": (tp + dt) % 4} for dx, dt in pairs]


def greet(peers):
    barrier = pltpu.get_barrier_semaphore()
    for peer in peers:
        pl.semaphore_signal(barrier, inc=1, device_id=peer, device_id_type=MESH)
    pl.semaphore_wait(barrier, len(peers))


class SeqGather:
    def __init__(self, own, blocks, send_sems, recv_sems):
        self.own, self.blocks = own, blocks
        self.send_sems, self.recv_sems = send_sems, recv_sems

    def send(self, slot, source, x, z, c, device):
        remote(
            source,
            self.blocks.at[x, z, c],
            self.send_sems.at[slot],
            self.recv_sems.at[x, z, c],
            device,
        ).start()

    def arrived(self, x, z, c):
        block = self.blocks.at[x, z, c]
        remote(
            block, block, self.send_sems.at[0], self.recv_sems.at[x, z, c], seq_peers()[-1]
        ).wait_recv()

    def start_z(self):
        x, z, c = place()
        for k, peer in enumerate(seq_peers()[:3]):
            self.send(k, self.own, x, z, c, peer)

    def start_x(self):
        x, z, c = place()
        for k, peer in enumerate(seq_peers()[3:]):
            self.send(3 + k, self.own, x, z, c, peer)

    def start(self):
        self.start_z()
        self.start_x()

    def forward_z(self):
        x, z, c = place()
        peers = seq_peers()
        for i, d in enumerate(OTHERS):
            from_z = (z + d) % 4
            self.arrived(x, from_z, c)
            for k, peer in enumerate(peers[3:]):
                self.send(7 + 4 * i + k, self.blocks.at[x, from_z, c], x, from_z, c, peer)

    def forward_x(self):
        x, z, c = place()
        partner = seq_peers()[-1]
        for i, dz in enumerate((0,) + OTHERS):
            for k, dx in enumerate(OTHERS):
                from_x, from_z = (x + dx) % 4, (z + dz) % 4
                self.arrived(from_x, from_z, c)
                block = self.blocks.at[from_x, from_z, c]
                self.send(19 + 3 * i + k, block, from_x, from_z, c, partner)

    def finish(self):
        x, z, c = place()
        for dz in (0,) + OTHERS:
            for dx in (0,) + OTHERS:
                self.arrived((x + dx) % 4, (z + dz) % 4, 1 - c)

    def drain(self):
        x, z, c = place()
        block = self.blocks.at[x, z, c]
        for slot in range(GATHER_SENDS):
            remote(
                block, block, self.send_sems.at[slot], self.recv_sems.at[x, z, c], seq_peers()[-1]
            ).wait_send()


GATHER_SENDS = 7 + 12 + 12


def head_norm_rope(values, gain, cosine, sine):
    lane = lax.broadcasted_iota(jnp.int32, (values.shape[0], 128), 1)
    low = lane < HEAD
    groups = []
    for g in range(values.shape[1] // 128):
        part = values[:, g * 128 : (g + 1) * 128]

        def average(t):
            first = jnp.sum(jnp.where(low, t, 0.0), axis=1, keepdims=True)
            second = jnp.sum(jnp.where(low, 0.0, t), axis=1, keepdims=True)
            return jnp.where(low, first, second) * (1.0 / HEAD)

        centred = part - average(part)
        unit = centred * lax.rsqrt(average(centred * centred) + 1e-06)
        unit = unit * gain
        turned = jnp.where(lane % 2 == 0, pltpu.roll(unit, 127, 1), pltpu.roll(unit, 1, 1))
        groups.append(unit * cosine + turned * sine)
    return jnp.concatenate(groups, axis=1)


def layer_kernel(
    hidden_ref,
    w_qkv_hbm,
    w_out_hbm,
    stale_ref,
    mod_ref,
    gain_ref,
    cos_ref,
    sin_ref,
    length_ref,
    out_ref,
    kv_ref,
    w_qkv,
    w_out,
    x_all,
    stale_all,
    fresh_keys,
    fresh_values,
    partial,
    reduced,
    mod_all,
    w_sems,
    x_send,
    x_recv,
    pass_send,
    r_send,
    r_recv,
    stale_send,
    stale_recv,
    key_send,
    key_recv,
    value_send,
    value_recv,
    mod_local,
    mod_send,
    column_recv,
    plane_recv,
):
    x, z, c = place()
    tp = lax.axis_index("tp")
    section = lax.axis_index("section")
    rows, share = hidden_ref.shape
    head_cols = w_qkv.shape[2]
    heads = head_cols // HEAD
    load_qkv = pltpu.make_async_copy(w_qkv_hbm, w_qkv, w_sems.at[0])
    load_out = pltpu.make_async_copy(w_out_hbm, w_out, w_sems.at[1])
    load_qkv.start()
    load_out.start()
    across = [{"section": 1 - section, "tp": (tp + d) % 4} for d in (0,) + OTHERS]
    greet(chip_column_peers() + plane_peers() + across)

    @pl.when(section == 0)
    def _():
        for k, peer in enumerate(tp_peers()):
            remote(hidden_ref, x_all.at[tp], x_send.at[k], x_recv.at[tp], peer).start()
        x_all[tp] = hidden_ref[...]

    keep = pltpu.make_async_copy(mod_ref, mod_all.at[x, tp, z, c], mod_local)
    keep.start()

    def column_copy(k, from_z, from_c):
        return remote(
            mod_ref,
            mod_all.at[x, tp, from_z, from_c],
            mod_send.at[k],
            column_recv.at[from_z, from_c],
            chip_column_peers()[k],
        )

    def plane_copy(k, from_x, from_tp):
        return remote(
            mod_all.at[from_x, from_tp],
            mod_all.at[from_x, from_tp],
            mod_send.at[7 + k],
            plane_recv.at[from_x, from_tp],
            plane_peers()[k],
        )

    for k in range(7):
        column_copy(k, z, c).start()
    stale = SeqGather(stale_ref, stale_all, stale_send, stale_recv)

    @pl.when(section == 0)
    def _():
        stale.start()

    stale_all[x, z, c] = stale_ref[...]
    keep.wait()
    for dz in (0,) + OTHERS:
        for dc in (0, 1):
            if (dz, dc) != (0, 0):
                column_copy(0, (z + dz) % 4, (c + dc) % 2).wait_recv()
    for k in range(15):
        plane_copy(k, x, tp).start()
    for dx in (0,) + OTHERS:
        for dt in (0,) + OTHERS:
            if (dx, dt) != (0, 0):
                plane_copy(0, (x + dx) % 4, (tp + dt) % 4).wait_recv()

    def x_arrived(source):
        remote(
            hidden_ref, x_all.at[source], x_send.at[0], x_recv.at[source], tp_peers()[0]
        ).wait_recv()

    @pl.when(section == 1)
    def _():
        stale.start()

    stale.forward_z()

    @pl.when(section == 1)
    def _():
        stale.forward_x()
        stale.finish()
        x_arrived(tp)

    for d in OTHERS:
        x_arrived((tp + d) % 4)

    token = lax.axis_index("seq") * rows + lax.broadcasted_iota(jnp.int32, (rows, 1), 0)
    video = token >= TEXT
    width = share * 4
    tiles = share // 128

    def mod_tile(row, index):
        group, step = divmod(row * (width // 128) + index, 9)
        found = None
        for member, half in ((step, 0), (step - 1, 1)):
            if 0 <= member < 8:
                at = (group // 4, member % 4, group % 4, member // 4, slice(half, half + 1))
                found = mod_all[at] if found is None else found + mod_all[at]
        return found

    def mod_rows(row, t):
        parts = [
            jnp.where(video, mod_tile(row, t * tiles + i), mod_tile(row + 3, t * tiles + i))
            for i in range(tiles)
        ]
        return jnp.concatenate(parts, axis=1)

    total = jnp.zeros((rows, 1), jnp.float32)
    for t in range(4):
        total += jnp.sum(x_all[t].astype(jnp.float32), axis=1, keepdims=True)
    mean = total * (1.0 / width)
    square = jnp.zeros((rows, 1), jnp.float32)
    for t in range(4):
        centred = x_all[t].astype(jnp.float32) - mean
        square += jnp.sum(centred * centred, axis=1, keepdims=True)
    inverse = lax.rsqrt(square * (1.0 / width) + 1e-05)
    load_qkv.wait()
    normed = []
    for t in range(4):
        centred = x_all[t].astype(jnp.float32) - mean
        scaled = centred * inverse * (1.0 + mod_rows(1, t)) + mod_rows(0, t)
        normed.append(scaled.astype(jnp.bfloat16))

    def project(part):
        proj = jnp.zeros((rows, head_cols), jnp.float32)
        for t in range(4):
            weights = w_qkv[part, t * share : (t + 1) * share, :]
            proj += jnp.dot(normed[t], weights, preferred_element_type=jnp.float32)
        return proj

    cosine, sine = cos_ref[...], sin_ref[...]
    gains = jnp.concatenate([gain_ref[...]] * 2, axis=1)
    keys = head_norm_rope(project(1), gains[1:2], cosine, sine).astype(jnp.bfloat16)
    kv_ref[0] = keys
    fresh_keys[x, z, c] = keys
    key_gather = SeqGather(kv_ref.at[0], fresh_keys, key_send, key_recv)
    key_gather.start()
    values = project(2).astype(jnp.bfloat16)
    kv_ref[1] = values
    fresh_values[x, z, c] = values
    value_gather = SeqGather(kv_ref.at[1], fresh_values, value_send, value_recv)
    value_gather.start()

    @pl.when(section == 0)
    def _():
        stale.forward_x()

    queries = head_norm_rope(project(0), gains[0:1], cosine, sine)
    stacked = jnp.concatenate([queries] * heads, axis=0)
    row_head = lax.broadcasted_iota(jnp.int32, stacked.shape, 0) // rows
    col_head = lax.broadcasted_iota(jnp.int32, stacked.shape, 1) // HEAD
    spread = jnp.where(row_head == col_head, stacked, 0.0).astype(jnp.bfloat16)
    key_gather.forward_z()
    value_gather.forward_z()

    @pl.when(section == 0)
    def _():
        stale.finish()

    tokens = rows * 32

    def all_rows(blocks):
        return blocks.reshape(tokens, head_cols)

    contract = (((1,), (1,)), ((), ()))
    scores_stale = lax.dot_general(
        spread, all_rows(stale_all[:, :, :, 0]), contract, preferred_element_type=jnp.float32
    )
    key_gather.forward_x()
    key_gather.finish()
    scores_fresh = lax.dot_general(
        spread, all_rows(fresh_keys[...]), contract, preferred_element_type=jnp.float32
    )
    column = lax.broadcasted_iota(jnp.int32, scores_fresh.shape, 1)
    first = TEXT + length_ref[0]
    second = first + length_ref[1]
    third = second + length_ref[2]
    limit = jnp.where(token < third, third, tokens)
    limit = jnp.where(token < first, first, jnp.where(token < second, second, limit))
    allowed = column < jnp.concatenate([limit] * heads, axis=0)
    scores = jnp.where(allowed, scores_fresh, scores_stale) * HEAD ** (-0.5)
    weights = jnp.exp(scores - jnp.max(scores, axis=1, keepdims=True))
    denominator = jnp.sum(weights, axis=1, keepdims=True)
    part_fresh = jnp.where(allowed, weights, 0.0).astype(jnp.bfloat16)
    part_stale = jnp.where(allowed, 0.0, weights).astype(jnp.bfloat16)
    mixed = jnp.dot(
        part_stale, all_rows(stale_all[:, :, :, 1]), preferred_element_type=jnp.float32
    )
    value_gather.forward_x()
    value_gather.finish()
    mixed += jnp.dot(part_fresh, all_rows(fresh_values[...]), preferred_element_type=jnp.float32)
    mixed = jnp.where(row_head == col_head, mixed / denominator, 0.0)
    attended = mixed[0:rows]
    for h in range(1, heads):
        attended += mixed[h * rows : (h + 1) * rows]
    attended = attended.astype(jnp.bfloat16)

    load_out.wait()
    for t in range(4):
        partial[t] = jnp.dot(
            attended, w_out[:, t * share : (t + 1) * share], preferred_element_type=jnp.float32
        ).astype(jnp.bfloat16)
    r_copies = []
    for k, d in enumerate(OTHERS):
        target = (tp + d) % 4
        copy = remote(
            partial.at[target], reduced.at[tp], r_send.at[k], r_recv.at[tp], {"tp": target}
        )
        copy.start()
        r_copies.append(copy)
    gate = jnp.zeros((rows, share), jnp.float32)
    for t in range(4):
        gate = jnp.where(tp == t, mod_rows(2, t), gate)
    projected = partial[tp].astype(jnp.float32)
    for k, d in enumerate(OTHERS):
        source = (tp + d) % 4
        remote(
            partial.at[source], reduced.at[source], r_send.at[k], r_recv.at[source], {"tp": source}
        ).wait_recv()
        projected += reduced[source].astype(jnp.float32)
    out_ref[...] = (x_all[tp].astype(jnp.float32) + gate * projected).astype(jnp.bfloat16)

    @pl.when(section == 0)
    def _():
        passes = []
        for k, peer in enumerate(across):
            copy = remote(out_ref, x_all.at[tp], pass_send.at[k], x_recv.at[tp], peer)
            copy.start()
            passes.append(copy)
        for k, peer in enumerate(tp_peers()):
            remote(hidden_ref, x_all.at[tp], x_send.at[k], x_recv.at[tp], peer).wait_send()
        for copy in passes:
            copy.wait_send()

    for copy in r_copies:
        copy.wait_send()
    for k in range(7):
        column_copy(k, z, c).wait_send()
    for k in range(15):
        plane_copy(k, x, tp).wait_send()
    stale.drain()
    key_gather.drain()
    value_gather.drain()


def run_layers(hidden, w_qkv, w_out, stale, modulate, gains, cosine, sine, lengths):
    rows, share = hidden.shape
    head_cols = w_out.shape[0]
    blocks = pltpu.VMEM((4, 4, 2, 2, rows, head_cols), jnp.bfloat16)
    half_blocks = pltpu.VMEM((4, 4, 2, rows, head_cols), jnp.bfloat16)
    dma = pltpu.SemaphoreType.DMA
    any_spec = pl.BlockSpec(memory_space=pl.ANY)
    return pl.pallas_call(
        layer_kernel,
        out_shape=(
            jax.ShapeDtypeStruct((rows, share), jnp.bfloat16),
            jax.ShapeDtypeStruct((2, rows, head_cols), jnp.bfloat16),
        ),
        in_specs=[VMEM_SPEC, any_spec, any_spec]
        + [VMEM_SPEC] * 5
        + [pl.BlockSpec(memory_space=pltpu.SMEM)],
        out_specs=(VMEM_SPEC, VMEM_SPEC),
        scratch_shapes=[
            pltpu.VMEM(w_qkv.shape, jnp.bfloat16),
            pltpu.VMEM(w_out.shape, jnp.bfloat16),
            pltpu.VMEM((4, rows, share), jnp.bfloat16),
            blocks,
            half_blocks,
            half_blocks,
            pltpu.VMEM((4, rows, share), jnp.bfloat16),
            pltpu.VMEM((4, rows, share), jnp.bfloat16),
            pltpu.VMEM((4, 4, 4, 2, 2, 128), jnp.float32),
            dma((2,)),
            dma((3,)),
            dma((4,)),
            dma((4,)),
            dma((3,)),
            dma((4,)),
            dma((GATHER_SENDS,)),
            dma((4, 4, 2)),
            dma((GATHER_SENDS,)),
            dma((4, 4, 2)),
            dma((GATHER_SENDS,)),
            dma((4, 4, 2)),
            dma,
            dma((22,)),
            dma((4, 2)),
            dma((4, 4)),
        ],
        compiler_params=pltpu.CompilerParams(collective_id=0, has_side_effects=True),
    )(hidden, w_qkv, w_out, stale, modulate, gains, cosine, sine, lengths)


def rope_tables(positions, first_row):
    column = jnp.arange(128)
    pair = (column % HEAD) // 2
    spans = ((0, HEAD // 4), (HEAD // 8, 3 * HEAD // 8), (5 * HEAD // 16, 3 * HEAD // 8))
    coords = positions.astype(jnp.float32)
    angles = jnp.zeros((positions.shape[1], 128), jnp.float32)
    for axis, (start, size) in enumerate(spans):
        exponent = 2.0 * (pair - start).astype(jnp.float32) / size
        inside = (pair >= start) & (pair < start + size // 2)
        frequency = jnp.where(inside, 1.0 / 10000.0**exponent, 0.0)
        angles = angles + coords[axis][:, None] * frequency[None, :]
    video = (first_row + jnp.arange(positions.shape[1]) >= TEXT)[:, None]
    sign = jnp.where(column % 2 == 0, -1.0, 1.0)[None, :]
    cosine = jnp.where(video, jnp.cos(angles), 1.0)
    return cosine, jnp.where(video, jnp.sin(angles) * sign, 0.0)


def local(
    hidden,
    qkv_weight,
    qk_gain,
    out_weight,
    mod_weight,
    stale_kv,
    patch_lengths,
    positions,
    timestep,
):
    tok_rows = hidden.shape[0]
    seq_rank = lax.axis_index("seq")
    share = jnp.dot(time_features(timestep), mod_weight[0], preferred_element_type=jnp.float32)
    device = seq_rank * lax.axis_size("tp") + lax.axis_index("tp")
    offset = (share.shape[1] * device) % 128
    placed = lax.dynamic_update_slice(jnp.zeros((1, 256), jnp.float32), share, (0, offset))
    cosine, sine = rope_tables(positions, seq_rank * tok_rows)
    result, fresh_kv = run_layers(
        hidden,
        jnp.transpose(qkv_weight[0], (1, 0, 2)),
        out_weight[0],
        stale_kv[0],
        placed.reshape(2, 128),
        qk_gain[0],
        cosine,
        sine,
        patch_lengths,
    )
    return (result[None], fresh_kv[None])


def solution(mesh):
    return jax.shard_map(
        local,
        mesh=mesh,
        in_specs=(
            P("seq", "tp"),
            P("section", None, None, "tp"),
            P("section", None, None),
            P("section", "tp", None),
            P("section", None, ("seq", "tp")),
            P("section", None, "seq", "tp"),
            P(),
            P(None, "seq"),
            P(),
        ),
        out_specs=(P("section", "seq", "tp"), P("section", None, "seq", "tp")),
        check_vma=False,
    )
```

```python
import math

import jax
import jax.numpy as jnp
from jax import lax
from jax.experimental import pallas as pl
from jax.experimental.pallas import tpu as pltpu
from jax.sharding import PartitionSpec as P

HEAD = 64
TEMB = 512
TEXT = 226


def time_features(timestep):
    half_width = TEMB // 2
    frequency = jnp.exp(
        -math.log(10000.0) * jnp.arange(half_width).astype(jnp.float32) / half_width
    )
    phases = timestep.astype(jnp.float32)[:, None] * frequency[None, :]
    embedded = jnp.concatenate([jnp.cos(phases), jnp.sin(phases)], axis=1)
    return jax.nn.silu(embedded).astype(jnp.bfloat16)


MESH = pl.DeviceIdType.MESH
OTHERS = (1, 3, 2)
VMEM_SPEC = pl.BlockSpec(memory_space=pltpu.VMEM)


def place():
    seq = lax.axis_index("seq")
    return seq // 8, (seq // 2) % 4, seq % 2


def seq_of(x, z, c):
    return (x * 4 + z) * 2 + c


def remote(source, target, send_sem, recv_sem, device):
    return pltpu.make_async_remote_copy(
        src_ref=source,
        dst_ref=target,
        send_sem=send_sem,
        recv_sem=recv_sem,
        device_id=device,
        device_id_type=MESH,
    )


def seq_peers():
    x, z, c = place()
    along_z = [{"seq": seq_of(x, (z + d) % 4, c)} for d in OTHERS]
    along_x = [{"seq": seq_of((x + d) % 4, z, c)} for d in OTHERS]
    return along_z + along_x + [{"seq": seq_of(x, z, 1 - c)}]


def tp_peers():
    tp = lax.axis_index("tp")
    return [{"tp": (tp + d) % 4} for d in OTHERS]


def chip_column_peers():
    x, z, c = place()
    pairs = [(dz, dc) for dz in (0,) + OTHERS for dc in (0, 1) if (dz, dc) != (0, 0)]
    return [{"seq": seq_of(x, (z + dz) % 4, (c + dc) % 2)} for dz, dc in pairs]


def plane_peers():
    x, z, c = place()
    tp = lax.axis_index("tp")
    pairs = [(dx, dt) for dx in (0,) + OTHERS for dt in (0,) + OTHERS if (dx, dt) != (0, 0)]
    return [{"seq": seq_of((x + dx) % 4, z, c), "tp": (tp + dt) % 4} for dx, dt in pairs]


def greet(peers):
    barrier = pltpu.get_barrier_semaphore()
    for peer in peers:
        pl.semaphore_signal(barrier, inc=1, device_id=peer, device_id_type=MESH)
    pl.semaphore_wait(barrier, len(peers))


def relay_order():
    c = lax.axis_index("seq") % 2
    return (3 - 2 * c, 1 + 2 * c, 2)


class SeqGather:
    def __init__(self, own, blocks, send_sems, recv_sems):
        self.own, self.blocks = own, blocks
        self.send_sems, self.recv_sems = send_sems, recv_sems

    def send(self, slot, source, x, z, c, device):
        remote(
            source,
            self.blocks.at[x, z, c],
            self.send_sems.at[slot],
            self.recv_sems.at[x, z, c],
            device,
        ).start()

    def arrived(self, x, z, c):
        block = self.blocks.at[x, z, c]
        remote(
            block, block, self.send_sems.at[0], self.recv_sems.at[x, z, c], seq_peers()[-1]
        ).wait_recv()

    def start(self):
        x, z, c = place()
        peers = seq_peers()
        for k, peer in enumerate(peers[:2] + peers[3:5] + peers[-1:]):
            self.send(k, self.own, x, z, c, peer)

    def forward_z(self):
        x, z, c = place()
        peers = seq_peers()
        slot = 5
        for i, d in enumerate(relay_order()):
            from_z = (z + d) % 4
            block = self.blocks.at[x, from_z, c]
            self.arrived(x, from_z, c)
            onward = [{"seq": seq_of(x, (z + 4 - d) % 4, c)}] if i == 0 else []
            for peer in onward + peers[3:5] + peers[-1:]:
                self.send(slot, block, x, from_z, c, peer)
                slot += 1

    def pass_x(self, i, d, slot):
        x, z, c = place()
        from_x = (x + d) % 4
        for dz in (0,) + relay_order():
            from_z = (z + dz) % 4
            block = self.blocks.at[from_x, from_z, c]
            self.arrived(from_x, from_z, c)
            onward = [{"seq": seq_of((x + 4 - d) % 4, z, c)}] if i == 0 else []
            for peer in onward + seq_peers()[-1:]:
                self.send(slot, block, from_x, from_z, c, peer)
                slot += 1

    def relay_x(self):
        self.pass_x(0, relay_order()[0], 15)

    def forward_x(self):
        self.pass_x(1, relay_order()[1], 23)
        self.pass_x(2, relay_order()[2], 27)

    def finish(self):
        x, z, c = place()
        for dz in (0,) + OTHERS:
            for dx in (0,) + OTHERS:
                self.arrived((x + dx) % 4, (z + dz) % 4, 1 - c)

    def drain(self):
        x, z, c = place()
        block = self.blocks.at[x, z, c]
        for slot in range(GATHER_SENDS):
            remote(
                block, block, self.send_sems.at[slot], self.recv_sems.at[x, z, c], seq_peers()[-1]
            ).wait_send()


GATHER_SENDS = 5 + 10 + 16


def head_norm_rope(values, gain, cosine, sine):
    lane = lax.broadcasted_iota(jnp.int32, (values.shape[0], 128), 1)
    low = lane < HEAD
    groups = []
    for g in range(values.shape[1] // 128):
        part = values[:, g * 128 : (g + 1) * 128]

        def average(t):
            first = jnp.sum(jnp.where(low, t, 0.0), axis=1, keepdims=True)
            second = jnp.sum(jnp.where(low, 0.0, t), axis=1, keepdims=True)
            return jnp.where(low, first, second) * (1.0 / HEAD)

        centred = part - average(part)
        unit = centred * lax.rsqrt(average(centred * centred) + 1e-06)
        unit = unit * gain
        turned = jnp.where(lane % 2 == 0, pltpu.roll(unit, 127, 1), pltpu.roll(unit, 1, 1))
        groups.append(unit * cosine + turned * sine)
    return jnp.concatenate(groups, axis=1)


def layer_kernel(
    hidden_ref,
    w_qkv_hbm,
    w_out_hbm,
    stale_ref,
    mod_ref,
    gain_ref,
    cos_ref,
    sin_ref,
    length_ref,
    out_ref,
    kv_ref,
    w_qkv,
    w_out,
    x_all,
    stale_all,
    fresh_keys,
    fresh_values,
    partial,
    reduced,
    mod_all,
    w_sems,
    x_send,
    x_recv,
    pass_send,
    r_send,
    r_recv,
    stale_send,
    stale_recv,
    key_send,
    key_recv,
    value_send,
    value_recv,
    mod_local,
    mod_send,
    column_recv,
    plane_recv,
):
    x, z, c = place()
    tp = lax.axis_index("tp")
    section = lax.axis_index("section")
    rows, share = hidden_ref.shape
    head_cols = w_qkv.shape[2]
    heads = head_cols // HEAD
    load_qkv = pltpu.make_async_copy(w_qkv_hbm, w_qkv, w_sems.at[0])
    load_out = pltpu.make_async_copy(w_out_hbm, w_out, w_sems.at[1])
    load_qkv.start()
    load_out.start()
    across = [{"section": 1 - section, "tp": (tp + d) % 4} for d in (0,) + OTHERS]
    greet(chip_column_peers() + plane_peers() + across)

    @pl.when(section == 0)
    def _():
        for k, peer in enumerate(tp_peers()):
            remote(hidden_ref, x_all.at[tp], x_send.at[k], x_recv.at[tp], peer).start()
        x_all[tp] = hidden_ref[...]

    keep = pltpu.make_async_copy(mod_ref, mod_all.at[x, tp, z, c], mod_local)
    keep.start()

    def column_copy(k, from_z, from_c):
        return remote(
            mod_ref,
            mod_all.at[x, tp, from_z, from_c],
            mod_send.at[k],
            column_recv.at[from_z, from_c],
            chip_column_peers()[k],
        )

    def plane_copy(k, from_x, from_tp):
        return remote(
            mod_all.at[from_x, from_tp],
            mod_all.at[from_x, from_tp],
            mod_send.at[7 + k],
            plane_recv.at[from_x, from_tp],
            plane_peers()[k],
        )

    for k in range(7):
        column_copy(k, z, c).start()
    stale = SeqGather(stale_ref, stale_all, stale_send, stale_recv)

    @pl.when(section == 0)
    def _():
        stale.start()

    stale_all[x, z, c] = stale_ref[...]
    keep.wait()
    for dz in (0,) + OTHERS:
        for dc in (0, 1):
            if (dz, dc) != (0, 0):
                column_copy(0, (z + dz) % 4, (c + dc) % 2).wait_recv()
    for k in range(15):
        plane_copy(k, x, tp).start()
    for dx in (0,) + OTHERS:
        for dt in (0,) + OTHERS:
            if (dx, dt) != (0, 0):
                plane_copy(0, (x + dx) % 4, (tp + dt) % 4).wait_recv()

    def x_arrived(source):
        remote(
            hidden_ref, x_all.at[source], x_send.at[0], x_recv.at[source], tp_peers()[0]
        ).wait_recv()

    @pl.when(section == 1)
    def _():
        stale.start()

    stale.forward_z()

    @pl.when(section == 1)
    def _():
        stale.relay_x()
        stale.forward_x()
        stale.finish()
        x_arrived(tp)

    for d in OTHERS:
        x_arrived((tp + d) % 4)

    token = lax.axis_index("seq") * rows + lax.broadcasted_iota(jnp.int32, (rows, 1), 0)
    video = token >= TEXT
    width = share * 4
    tiles = share // 128

    def mod_tile(row, index):
        group, step = divmod(row * (width // 128) + index, 9)
        found = None
        for member, half in ((step, 0), (step - 1, 1)):
            if 0 <= member < 8:
                at = (group // 4, member % 4, group % 4, member // 4, slice(half, half + 1))
                found = mod_all[at] if found is None else found + mod_all[at]
        return found

    def mod_rows(row, t):
        parts = [
            jnp.where(video, mod_tile(row, t * tiles + i), mod_tile(row + 3, t * tiles + i))
            for i in range(tiles)
        ]
        return jnp.concatenate(parts, axis=1)

    total = jnp.zeros((rows, 1), jnp.float32)
    for t in range(4):
        total += jnp.sum(x_all[t].astype(jnp.float32), axis=1, keepdims=True)
    mean = total * (1.0 / width)
    square = jnp.zeros((rows, 1), jnp.float32)
    for t in range(4):
        centred = x_all[t].astype(jnp.float32) - mean
        square += jnp.sum(centred * centred, axis=1, keepdims=True)
    inverse = lax.rsqrt(square * (1.0 / width) + 1e-05)
    load_qkv.wait()
    normed = []
    for t in range(4):
        centred = x_all[t].astype(jnp.float32) - mean
        scaled = centred * inverse * (1.0 + mod_rows(1, t)) + mod_rows(0, t)
        normed.append(scaled.astype(jnp.bfloat16))

    def project(part):
        proj = jnp.zeros((rows, head_cols), jnp.float32)
        for t in range(4):
            weights = w_qkv[part, t * share : (t + 1) * share, :]
            proj += jnp.dot(normed[t], weights, preferred_element_type=jnp.float32)
        return proj

    cosine, sine = cos_ref[...], sin_ref[...]
    gains = jnp.concatenate([gain_ref[...]] * 2, axis=1)
    keys = head_norm_rope(project(1), gains[1:2], cosine, sine).astype(jnp.bfloat16)
    kv_ref[0] = keys
    fresh_keys[x, z, c] = keys
    key_gather = SeqGather(kv_ref.at[0], fresh_keys, key_send, key_recv)
    key_gather.start()
    values = project(2).astype(jnp.bfloat16)
    kv_ref[1] = values
    fresh_values[x, z, c] = values
    value_gather = SeqGather(kv_ref.at[1], fresh_values, value_send, value_recv)
    value_gather.start()

    queries = head_norm_rope(project(0), gains[0:1], cosine, sine)
    stacked = jnp.concatenate([queries] * heads, axis=0)
    row_head = lax.broadcasted_iota(jnp.int32, stacked.shape, 0) // rows
    col_head = lax.broadcasted_iota(jnp.int32, stacked.shape, 1) // HEAD
    spread = jnp.where(row_head == col_head, stacked, 0.0).astype(jnp.bfloat16)

    @pl.when(section == 0)
    def _():
        stale.relay_x()

    key_gather.forward_z()
    value_gather.forward_z()

    @pl.when(section == 0)
    def _():
        stale.forward_x()
        stale.finish()

    key_gather.relay_x()

    tokens = rows * 32

    def all_rows(blocks):
        return blocks.reshape(tokens, head_cols)

    contract = (((1,), (1,)), ((), ()))
    scores_stale = lax.dot_general(
        spread, all_rows(stale_all[:, :, :, 0]), contract, preferred_element_type=jnp.float32
    )
    key_gather.forward_x()
    key_gather.finish()
    value_gather.relay_x()
    scores_fresh = lax.dot_general(
        spread, all_rows(fresh_keys[...]), contract, preferred_element_type=jnp.float32
    )
    column = lax.broadcasted_iota(jnp.int32, scores_fresh.shape, 1)
    first = TEXT + length_ref[0]
    second = first + length_ref[1]
    third = second + length_ref[2]
    limit = jnp.where(token < third, third, tokens)
    limit = jnp.where(token < first, first, jnp.where(token < second, second, limit))
    allowed = column < jnp.concatenate([limit] * heads, axis=0)
    scores = jnp.where(allowed, scores_fresh, scores_stale) * HEAD ** (-0.5)
    weights = jnp.exp(scores - jnp.max(scores, axis=1, keepdims=True))
    denominator = jnp.sum(weights, axis=1, keepdims=True)
    part_fresh = jnp.where(allowed, weights, 0.0).astype(jnp.bfloat16)
    part_stale = jnp.where(allowed, 0.0, weights).astype(jnp.bfloat16)
    mixed = jnp.dot(
        part_stale, all_rows(stale_all[:, :, :, 1]), preferred_element_type=jnp.float32
    )
    value_gather.forward_x()
    value_gather.finish()
    mixed += jnp.dot(part_fresh, all_rows(fresh_values[...]), preferred_element_type=jnp.float32)
    mixed = jnp.where(row_head == col_head, mixed / denominator, 0.0)
    attended = mixed[0:rows]
    for h in range(1, heads):
        attended += mixed[h * rows : (h + 1) * rows]
    attended = attended.astype(jnp.bfloat16)

    load_out.wait()
    for t in range(4):
        partial[t] = jnp.dot(
            attended, w_out[:, t * share : (t + 1) * share], preferred_element_type=jnp.float32
        ).astype(jnp.bfloat16)
    r_copies = []
    for k, d in enumerate(OTHERS):
        target = (tp + d) % 4
        copy = remote(
            partial.at[target], reduced.at[tp], r_send.at[k], r_recv.at[tp], {"tp": target}
        )
        copy.start()
        r_copies.append(copy)
    gate = jnp.zeros((rows, share), jnp.float32)
    for t in range(4):
        gate = jnp.where(tp == t, mod_rows(2, t), gate)
    projected = partial[tp].astype(jnp.float32)
    for k, d in enumerate(OTHERS):
        source = (tp + d) % 4
        remote(
            partial.at[source], reduced.at[source], r_send.at[k], r_recv.at[source], {"tp": source}
        ).wait_recv()
        projected += reduced[source].astype(jnp.float32)
    out_ref[...] = (x_all[tp].astype(jnp.float32) + gate * projected).astype(jnp.bfloat16)

    @pl.when(section == 0)
    def _():
        passes = []
        for k, peer in enumerate(across):
            copy = remote(out_ref, x_all.at[tp], pass_send.at[k], x_recv.at[tp], peer)
            copy.start()
            passes.append(copy)
        for k, peer in enumerate(tp_peers()):
            remote(hidden_ref, x_all.at[tp], x_send.at[k], x_recv.at[tp], peer).wait_send()
        for copy in passes:
            copy.wait_send()

    for copy in r_copies:
        copy.wait_send()
    for k in range(7):
        column_copy(k, z, c).wait_send()
    for k in range(15):
        plane_copy(k, x, tp).wait_send()
    stale.drain()
    key_gather.drain()
    value_gather.drain()


def run_layers(hidden, w_qkv, w_out, stale, modulate, gains, cosine, sine, lengths):
    rows, share = hidden.shape
    head_cols = w_out.shape[0]
    blocks = pltpu.VMEM((4, 4, 2, 2, rows, head_cols), jnp.bfloat16)
    half_blocks = pltpu.VMEM((4, 4, 2, rows, head_cols), jnp.bfloat16)
    dma = pltpu.SemaphoreType.DMA
    any_spec = pl.BlockSpec(memory_space=pl.ANY)
    return pl.pallas_call(
        layer_kernel,
        out_shape=(
            jax.ShapeDtypeStruct((rows, share), jnp.bfloat16),
            jax.ShapeDtypeStruct((2, rows, head_cols), jnp.bfloat16),
        ),
        in_specs=[VMEM_SPEC, any_spec, any_spec]
        + [VMEM_SPEC] * 5
        + [pl.BlockSpec(memory_space=pltpu.SMEM)],
        out_specs=(VMEM_SPEC, VMEM_SPEC),
        scratch_shapes=[
            pltpu.VMEM(w_qkv.shape, jnp.bfloat16),
            pltpu.VMEM(w_out.shape, jnp.bfloat16),
            pltpu.VMEM((4, rows, share), jnp.bfloat16),
            blocks,
            half_blocks,
            half_blocks,
            pltpu.VMEM((4, rows, share), jnp.bfloat16),
            pltpu.VMEM((4, rows, share), jnp.bfloat16),
            pltpu.VMEM((4, 4, 4, 2, 2, 128), jnp.float32),
            dma((2,)),
            dma((3,)),
            dma((4,)),
            dma((4,)),
            dma((3,)),
            dma((4,)),
            dma((GATHER_SENDS,)),
            dma((4, 4, 2)),
            dma((GATHER_SENDS,)),
            dma((4, 4, 2)),
            dma((GATHER_SENDS,)),
            dma((4, 4, 2)),
            dma,
            dma((22,)),
            dma((4, 2)),
            dma((4, 4)),
        ],
        compiler_params=pltpu.CompilerParams(collective_id=0, has_side_effects=True),
    )(hidden, w_qkv, w_out, stale, modulate, gains, cosine, sine, lengths)


def rope_tables(positions, first_row):
    column = jnp.arange(128)
    pair = (column % HEAD) // 2
    spans = ((0, HEAD // 4), (HEAD // 8, 3 * HEAD // 8), (5 * HEAD // 16, 3 * HEAD // 8))
    coords = positions.astype(jnp.float32)
    angles = jnp.zeros((positions.shape[1], 128), jnp.float32)
    for axis, (start, size) in enumerate(spans):
        exponent = 2.0 * (pair - start).astype(jnp.float32) / size
        inside = (pair >= start) & (pair < start + size // 2)
        frequency = jnp.where(inside, 1.0 / 10000.0**exponent, 0.0)
        angles = angles + coords[axis][:, None] * frequency[None, :]
    video = (first_row + jnp.arange(positions.shape[1]) >= TEXT)[:, None]
    sign = jnp.where(column % 2 == 0, -1.0, 1.0)[None, :]
    cosine = jnp.where(video, jnp.cos(angles), 1.0)
    return cosine, jnp.where(video, jnp.sin(angles) * sign, 0.0)


def local(
    hidden,
    qkv_weight,
    qk_gain,
    out_weight,
    mod_weight,
    stale_kv,
    patch_lengths,
    positions,
    timestep,
):
    tok_rows = hidden.shape[0]
    seq_rank = lax.axis_index("seq")
    share = jnp.dot(time_features(timestep), mod_weight[0], preferred_element_type=jnp.float32)
    device = seq_rank * lax.axis_size("tp") + lax.axis_index("tp")
    offset = (share.shape[1] * device) % 128
    placed = lax.dynamic_update_slice(jnp.zeros((1, 256), jnp.float32), share, (0, offset))
    cosine, sine = rope_tables(positions, seq_rank * tok_rows)
    result, fresh_kv = run_layers(
        hidden,
        jnp.transpose(qkv_weight[0], (1, 0, 2)),
        out_weight[0],
        stale_kv[0],
        placed.reshape(2, 128),
        qk_gain[0],
        cosine,
        sine,
        patch_lengths,
    )
    return (result[None], fresh_kv[None])


def solution(mesh):
    return jax.shard_map(
        local,
        mesh=mesh,
        in_specs=(
            P("seq", "tp"),
            P("section", None, None, "tp"),
            P("section", None, None),
            P("section", "tp", None),
            P("section", None, ("seq", "tp")),
            P("section", None, "seq", "tp"),
            P(),
            P(None, "seq"),
            P(),
        ),
        out_specs=(P("section", "seq", "tp"), P("section", None, "seq", "tp")),
        check_vma=False,
    )
```

```python
import math

import jax
import jax.numpy as jnp
from jax import lax
from jax.experimental import pallas as pl
from jax.experimental.pallas import tpu as pltpu
from jax.sharding import PartitionSpec as P

HEAD = 64
TEMB = 512
TEXT = 226


def time_features(timestep):
    half_width = TEMB // 2
    frequency = jnp.exp(
        -math.log(10000.0) * jnp.arange(half_width).astype(jnp.float32) / half_width
    )
    phases = timestep.astype(jnp.float32)[:, None] * frequency[None, :]
    embedded = jnp.concatenate([jnp.cos(phases), jnp.sin(phases)], axis=1)
    return jax.nn.silu(embedded).astype(jnp.bfloat16)


MESH = pl.DeviceIdType.MESH
OTHERS = (1, 3, 2)
VMEM_SPEC = pl.BlockSpec(memory_space=pltpu.VMEM)


def place():
    seq = lax.axis_index("seq")
    return seq // 8, (seq // 2) % 4, seq % 2


def seq_of(x, z, c):
    return (x * 4 + z) * 2 + c


def remote(source, target, send_sem, recv_sem, device):
    return pltpu.make_async_remote_copy(
        src_ref=source,
        dst_ref=target,
        send_sem=send_sem,
        recv_sem=recv_sem,
        device_id=device,
        device_id_type=MESH,
    )


def seq_peers():
    x, z, c = place()
    along_z = [{"seq": seq_of(x, (z + d) % 4, c)} for d in OTHERS]
    along_x = [{"seq": seq_of((x + d) % 4, z, c)} for d in OTHERS]
    return along_z + along_x + [{"seq": seq_of(x, z, 1 - c)}]


def tp_peers():
    tp = lax.axis_index("tp")
    return [{"tp": (tp + d) % 4} for d in OTHERS]


def chip_column_peers():
    x, z, c = place()
    pairs = [(dz, dc) for dz in (0,) + OTHERS for dc in (0, 1) if (dz, dc) != (0, 0)]
    return [{"seq": seq_of(x, (z + dz) % 4, (c + dc) % 2)} for dz, dc in pairs]


def plane_peers():
    x, z, c = place()
    tp = lax.axis_index("tp")
    pairs = [(dx, dt) for dx in (0,) + OTHERS for dt in (0,) + OTHERS if (dx, dt) != (0, 0)]
    return [{"seq": seq_of((x + dx) % 4, z, c), "tp": (tp + dt) % 4} for dx, dt in pairs]


def greet(peers):
    barrier = pltpu.get_barrier_semaphore()
    for peer in peers:
        pl.semaphore_signal(barrier, inc=1, device_id=peer, device_id_type=MESH)
    pl.semaphore_wait(barrier, len(peers))


class SeqGather:
    def __init__(self, own, blocks, send_sems, recv_sems):
        self.own, self.blocks = own, blocks
        self.send_sems, self.recv_sems = send_sems, recv_sems

    def send(self, slot, source, x, z, c, device):
        remote(
            source,
            self.blocks.at[x, z, c],
            self.send_sems.at[slot],
            self.recv_sems.at[x, z, c],
            device,
        ).start()

    def arrived(self, x, z, c):
        block = self.blocks.at[x, z, c]
        remote(
            block, block, self.send_sems.at[0], self.recv_sems.at[x, z, c], seq_peers()[-1]
        ).wait_recv()

    def start_z(self):
        x, z, c = place()
        for k, peer in enumerate(seq_peers()[:3]):
            self.send(k, self.own, x, z, c, peer)

    def start_x(self):
        x, z, c = place()
        for k, peer in enumerate(seq_peers()[3:]):
            self.send(3 + k, self.own, x, z, c, peer)

    def start(self):
        self.start_z()
        self.start_x()

    def forward_z(self):
        x, z, c = place()
        peers = seq_peers()
        for i, d in enumerate(OTHERS):
            from_z = (z + d) % 4
            self.arrived(x, from_z, c)
            for k, peer in enumerate(peers[3:]):
                self.send(7 + 4 * i + k, self.blocks.at[x, from_z, c], x, from_z, c, peer)

    def forward_x(self):
        x, z, c = place()
        partner = seq_peers()[-1]
        for i, dz in enumerate((0,) + OTHERS):
            for k, dx in enumerate(OTHERS):
                from_x, from_z = (x + dx) % 4, (z + dz) % 4
                self.arrived(from_x, from_z, c)
                block = self.blocks.at[from_x, from_z, c]
                self.send(19 + 3 * i + k, block, from_x, from_z, c, partner)

    def finish(self):
        x, z, c = place()
        for dz in (0,) + OTHERS:
            for dx in (0,) + OTHERS:
                self.arrived((x + dx) % 4, (z + dz) % 4, 1 - c)

    def drain(self):
        x, z, c = place()
        block = self.blocks.at[x, z, c]
        for slot in range(GATHER_SENDS):
            remote(
                block, block, self.send_sems.at[slot], self.recv_sems.at[x, z, c], seq_peers()[-1]
            ).wait_send()


GATHER_SENDS = 7 + 12 + 12


def head_norm_rope(values, gain, cosine, sine):
    lane = lax.broadcasted_iota(jnp.int32, (values.shape[0], 128), 1)
    low = lane < HEAD
    groups = []
    for g in range(values.shape[1] // 128):
        part = values[:, g * 128 : (g + 1) * 128]

        def average(t):
            first = jnp.sum(jnp.where(low, t, 0.0), axis=1, keepdims=True)
            second = jnp.sum(jnp.where(low, 0.0, t), axis=1, keepdims=True)
            return jnp.where(low, first, second) * (1.0 / HEAD)

        centred = part - average(part)
        unit = centred * lax.rsqrt(average(centred * centred) + 1e-06)
        unit = unit * gain
        turned = jnp.where(lane % 2 == 0, pltpu.roll(unit, 127, 1), pltpu.roll(unit, 1, 1))
        groups.append(unit * cosine + turned * sine)
    return jnp.concatenate(groups, axis=1)


def layer_kernel(
    hidden_ref,
    w_qkv_hbm,
    w_out_hbm,
    stale_ref,
    mod_ref,
    gain_ref,
    cos_ref,
    sin_ref,
    length_ref,
    out_ref,
    kv_ref,
    w_qkv,
    w_out,
    x_all,
    stale_all,
    fresh_keys,
    fresh_values,
    partial,
    reduced,
    mod_all,
    w_sems,
    x_send,
    x_recv,
    pass_send,
    r_send,
    r_recv,
    stale_send,
    stale_recv,
    key_send,
    key_recv,
    value_send,
    value_recv,
    mod_local,
    mod_send,
    column_recv,
    plane_recv,
):
    x, z, c = place()
    tp = lax.axis_index("tp")
    section = lax.axis_index("section")
    rows, share = hidden_ref.shape
    head_cols = w_qkv.shape[2]
    heads = head_cols // HEAD
    load_qkv = pltpu.make_async_copy(w_qkv_hbm, w_qkv, w_sems.at[0])
    load_out = pltpu.make_async_copy(w_out_hbm, w_out, w_sems.at[1])
    load_qkv.start()
    load_out.start()
    across = [{"section": 1 - section, "tp": (tp + d) % 4} for d in (0,) + OTHERS]
    greet(chip_column_peers() + plane_peers() + across)

    @pl.when(section == 0)
    def _():
        for k, peer in enumerate(tp_peers()):
            remote(hidden_ref, x_all.at[tp], x_send.at[k], x_recv.at[tp], peer).start()
        x_all[tp] = hidden_ref[...]

    keep = pltpu.make_async_copy(mod_ref, mod_all.at[x, tp, z, c], mod_local)
    keep.start()

    def column_copy(k, from_z, from_c):
        return remote(
            mod_ref,
            mod_all.at[x, tp, from_z, from_c],
            mod_send.at[k],
            column_recv.at[from_z, from_c],
            chip_column_peers()[k],
        )

    def plane_copy(k, from_x, from_tp):
        return remote(
            mod_all.at[from_x, from_tp],
            mod_all.at[from_x, from_tp],
            mod_send.at[7 + k],
            plane_recv.at[from_x, from_tp],
            plane_peers()[k],
        )

    for k in range(7):
        column_copy(k, z, c).start()
    stale = SeqGather(stale_ref, stale_all, stale_send, stale_recv)

    @pl.when(section == 0)
    def _():
        stale.start()

    stale_all[x, z, c] = stale_ref[...]
    keep.wait()
    for dz in (0,) + OTHERS:
        for dc in (0, 1):
            if (dz, dc) != (0, 0):
                column_copy(0, (z + dz) % 4, (c + dc) % 2).wait_recv()
    for k in range(15):
        plane_copy(k, x, tp).start()
    for dx in (0,) + OTHERS:
        for dt in (0,) + OTHERS:
            if (dx, dt) != (0, 0):
                plane_copy(0, (x + dx) % 4, (tp + dt) % 4).wait_recv()

    def x_arrived(source):
        remote(
            hidden_ref, x_all.at[source], x_send.at[0], x_recv.at[source], tp_peers()[0]
        ).wait_recv()

    @pl.when(section == 1)
    def _():
        stale.start()

    stale.forward_z()

    @pl.when(section == 1)
    def _():
        stale.forward_x()
        stale.finish()
        x_arrived(tp)

    for d in OTHERS:
        x_arrived((tp + d) % 4)

    token = lax.axis_index("seq") * rows + lax.broadcasted_iota(jnp.int32, (rows, 1), 0)
    video = token >= TEXT
    width = share * 4
    tiles = share // 128

    def mod_tile(row, index):
        group, step = divmod(row * (width // 128) + index, 9)
        found = None
        for member, half in ((step, 0), (step - 1, 1)):
            if 0 <= member < 8:
                at = (group // 4, member % 4, group % 4, member // 4, slice(half, half + 1))
                found = mod_all[at] if found is None else found + mod_all[at]
        return found

    def mod_rows(row, t):
        parts = [
            jnp.where(video, mod_tile(row, t * tiles + i), mod_tile(row + 3, t * tiles + i))
            for i in range(tiles)
        ]
        return jnp.concatenate(parts, axis=1)

    total = jnp.zeros((rows, 1), jnp.float32)
    for t in range(4):
        total += jnp.sum(x_all[t].astype(jnp.float32), axis=1, keepdims=True)
    mean = total * (1.0 / width)
    square = jnp.zeros((rows, 1), jnp.float32)
    for t in range(4):
        centred = x_all[t].astype(jnp.float32) - mean
        square += jnp.sum(centred * centred, axis=1, keepdims=True)
    inverse = lax.rsqrt(square * (1.0 / width) + 1e-05)
    load_qkv.wait()
    normed = []
    for t in range(4):
        centred = x_all[t].astype(jnp.float32) - mean
        scaled = centred * inverse * (1.0 + mod_rows(1, t)) + mod_rows(0, t)
        normed.append(scaled.astype(jnp.bfloat16))

    def project(part):
        proj = jnp.zeros((rows, head_cols), jnp.float32)
        for t in range(4):
            weights = w_qkv[part, t * share : (t + 1) * share, :]
            proj += jnp.dot(normed[t], weights, preferred_element_type=jnp.float32)
        return proj

    cosine, sine = cos_ref[...], sin_ref[...]
    gains = jnp.concatenate([gain_ref[...]] * 2, axis=1)
    keys = head_norm_rope(project(1), gains[1:2], cosine, sine).astype(jnp.bfloat16)
    kv_ref[0] = keys
    fresh_keys[x, z, c] = keys
    key_gather = SeqGather(kv_ref.at[0], fresh_keys, key_send, key_recv)
    key_gather.start()
    values = project(2).astype(jnp.bfloat16)
    kv_ref[1] = values
    fresh_values[x, z, c] = values
    value_gather = SeqGather(kv_ref.at[1], fresh_values, value_send, value_recv)
    value_gather.start()

    queries = head_norm_rope(project(0), gains[0:1], cosine, sine)
    stacked = jnp.concatenate([queries] * heads, axis=0)
    row_head = lax.broadcasted_iota(jnp.int32, stacked.shape, 0) // rows
    col_head = lax.broadcasted_iota(jnp.int32, stacked.shape, 1) // HEAD
    spread = jnp.where(row_head == col_head, stacked, 0.0).astype(jnp.bfloat16)
    key_gather.forward_z()
    value_gather.forward_z()

    @pl.when(section == 0)
    def _():
        stale.forward_x()

    key_gather.forward_x()

    @pl.when(section == 0)
    def _():
        stale.finish()

    tokens = rows * 32

    def all_rows(blocks):
        return blocks.reshape(tokens, head_cols)

    contract = (((1,), (1,)), ((), ()))
    scores_stale = lax.dot_general(
        spread, all_rows(stale_all[:, :, :, 0]), contract, preferred_element_type=jnp.float32
    )
    key_gather.finish()
    scores_fresh = lax.dot_general(
        spread, all_rows(fresh_keys[...]), contract, preferred_element_type=jnp.float32
    )
    column = lax.broadcasted_iota(jnp.int32, scores_fresh.shape, 1)
    first = TEXT + length_ref[0]
    second = first + length_ref[1]
    third = second + length_ref[2]
    limit = jnp.where(token < third, third, tokens)
    limit = jnp.where(token < first, first, jnp.where(token < second, second, limit))
    allowed = column < jnp.concatenate([limit] * heads, axis=0)
    scores = jnp.where(allowed, scores_fresh, scores_stale) * HEAD ** (-0.5)
    weights = jnp.exp(scores - jnp.max(scores, axis=1, keepdims=True))
    denominator = jnp.sum(weights, axis=1, keepdims=True)
    part_fresh = jnp.where(allowed, weights, 0.0).astype(jnp.bfloat16)
    part_stale = jnp.where(allowed, 0.0, weights).astype(jnp.bfloat16)
    value_gather.forward_x()
    mixed = jnp.dot(
        part_stale, all_rows(stale_all[:, :, :, 1]), preferred_element_type=jnp.float32
    )
    value_gather.finish()
    mixed += jnp.dot(part_fresh, all_rows(fresh_values[...]), preferred_element_type=jnp.float32)
    mixed = jnp.where(row_head == col_head, mixed / denominator, 0.0)
    attended = mixed[0:rows]
    for h in range(1, heads):
        attended += mixed[h * rows : (h + 1) * rows]
    attended = attended.astype(jnp.bfloat16)

    load_out.wait()
    for t in range(4):
        partial[t] = jnp.dot(
            attended, w_out[:, t * share : (t + 1) * share], preferred_element_type=jnp.float32
        ).astype(jnp.bfloat16)
    r_copies = []
    for k, d in enumerate(OTHERS):
        target = (tp + d) % 4
        copy = remote(
            partial.at[target], reduced.at[tp], r_send.at[k], r_recv.at[tp], {"tp": target}
        )
        copy.start()
        r_copies.append(copy)
    gate = jnp.zeros((rows, share), jnp.float32)
    for t in range(4):
        gate = jnp.where(tp == t, mod_rows(2, t), gate)
    projected = partial[tp].astype(jnp.float32)
    for k, d in enumerate(OTHERS):
        source = (tp + d) % 4
        remote(
            partial.at[source], reduced.at[source], r_send.at[k], r_recv.at[source], {"tp": source}
        ).wait_recv()
        projected += reduced[source].astype(jnp.float32)
    out_ref[...] = (x_all[tp].astype(jnp.float32) + gate * projected).astype(jnp.bfloat16)

    @pl.when(section == 0)
    def _():
        passes = []
        for k, peer in enumerate(across):
            copy = remote(out_ref, x_all.at[tp], pass_send.at[k], x_recv.at[tp], peer)
            copy.start()
            passes.append(copy)
        for k, peer in enumerate(tp_peers()):
            remote(hidden_ref, x_all.at[tp], x_send.at[k], x_recv.at[tp], peer).wait_send()
        for copy in passes:
            copy.wait_send()

    for copy in r_copies:
        copy.wait_send()
    for k in range(7):
        column_copy(k, z, c).wait_send()
    for k in range(15):
        plane_copy(k, x, tp).wait_send()
    stale.drain()
    key_gather.drain()
    value_gather.drain()


def run_layers(hidden, w_qkv, w_out, stale, modulate, gains, cosine, sine, lengths):
    rows, share = hidden.shape
    head_cols = w_out.shape[0]
    blocks = pltpu.VMEM((4, 4, 2, 2, rows, head_cols), jnp.bfloat16)
    half_blocks = pltpu.VMEM((4, 4, 2, rows, head_cols), jnp.bfloat16)
    dma = pltpu.SemaphoreType.DMA
    any_spec = pl.BlockSpec(memory_space=pl.ANY)
    return pl.pallas_call(
        layer_kernel,
        out_shape=(
            jax.ShapeDtypeStruct((rows, share), jnp.bfloat16),
            jax.ShapeDtypeStruct((2, rows, head_cols), jnp.bfloat16),
        ),
        in_specs=[VMEM_SPEC, any_spec, any_spec]
        + [VMEM_SPEC] * 5
        + [pl.BlockSpec(memory_space=pltpu.SMEM)],
        out_specs=(VMEM_SPEC, VMEM_SPEC),
        scratch_shapes=[
            pltpu.VMEM(w_qkv.shape, jnp.bfloat16),
            pltpu.VMEM(w_out.shape, jnp.bfloat16),
            pltpu.VMEM((4, rows, share), jnp.bfloat16),
            blocks,
            half_blocks,
            half_blocks,
            pltpu.VMEM((4, rows, share), jnp.bfloat16),
            pltpu.VMEM((4, rows, share), jnp.bfloat16),
            pltpu.VMEM((4, 4, 4, 2, 2, 128), jnp.float32),
            dma((2,)),
            dma((3,)),
            dma((4,)),
            dma((4,)),
            dma((3,)),
            dma((4,)),
            dma((GATHER_SENDS,)),
            dma((4, 4, 2)),
            dma((GATHER_SENDS,)),
            dma((4, 4, 2)),
            dma((GATHER_SENDS,)),
            dma((4, 4, 2)),
            dma,
            dma((22,)),
            dma((4, 2)),
            dma((4, 4)),
        ],
        compiler_params=pltpu.CompilerParams(collective_id=0, has_side_effects=True),
    )(hidden, w_qkv, w_out, stale, modulate, gains, cosine, sine, lengths)


def rope_tables(positions, first_row):
    column = jnp.arange(128)
    pair = (column % HEAD) // 2
    spans = ((0, HEAD // 4), (HEAD // 8, 3 * HEAD // 8), (5 * HEAD // 16, 3 * HEAD // 8))
    coords = positions.astype(jnp.float32)
    angles = jnp.zeros((positions.shape[1], 128), jnp.float32)
    for axis, (start, size) in enumerate(spans):
        exponent = 2.0 * (pair - start).astype(jnp.float32) / size
        inside = (pair >= start) & (pair < start + size // 2)
        frequency = jnp.where(inside, 1.0 / 10000.0**exponent, 0.0)
        angles = angles + coords[axis][:, None] * frequency[None, :]
    video = (first_row + jnp.arange(positions.shape[1]) >= TEXT)[:, None]
    sign = jnp.where(column % 2 == 0, -1.0, 1.0)[None, :]
    cosine = jnp.where(video, jnp.cos(angles), 1.0)
    return cosine, jnp.where(video, jnp.sin(angles) * sign, 0.0)


def local(
    hidden,
    qkv_weight,
    qk_gain,
    out_weight,
    mod_weight,
    stale_kv,
    patch_lengths,
    positions,
    timestep,
):
    tok_rows = hidden.shape[0]
    seq_rank = lax.axis_index("seq")
    share = jnp.dot(time_features(timestep), mod_weight[0], preferred_element_type=jnp.float32)
    device = seq_rank * lax.axis_size("tp") + lax.axis_index("tp")
    offset = (share.shape[1] * device) % 128
    placed = lax.dynamic_update_slice(jnp.zeros((1, 256), jnp.float32), share, (0, offset))
    cosine, sine = rope_tables(positions, seq_rank * tok_rows)
    result, fresh_kv = run_layers(
        hidden,
        jnp.transpose(qkv_weight[0], (1, 0, 2)),
        out_weight[0],
        stale_kv[0],
        placed.reshape(2, 128),
        qk_gain[0],
        cosine,
        sine,
        patch_lengths,
    )
    return (result[None], fresh_kv[None])


def solution(mesh):
    return jax.shard_map(
        local,
        mesh=mesh,
        in_specs=(
            P("seq", "tp"),
            P("section", None, None, "tp"),
            P("section", None, None),
            P("section", "tp", None),
            P("section", None, ("seq", "tp")),
            P("section", None, "seq", "tp"),
            P(),
            P(None, "seq"),
            P(),
        ),
        out_specs=(P("section", "seq", "tp"), P("section", None, "seq", "tp")),
        check_vma=False,
    )
```

```python
import math

import jax
import jax.numpy as jnp
from jax import lax
from jax.experimental import pallas as pl
from jax.experimental.pallas import tpu as pltpu
from jax.sharding import PartitionSpec as P

HEAD = 64
TEMB = 512
TEXT = 226


def time_features(timestep):
    half_width = TEMB // 2
    frequency = jnp.exp(
        -math.log(10000.0) * jnp.arange(half_width).astype(jnp.float32) / half_width
    )
    phases = timestep.astype(jnp.float32)[:, None] * frequency[None, :]
    embedded = jnp.concatenate([jnp.cos(phases), jnp.sin(phases)], axis=1)
    return jax.nn.silu(embedded).astype(jnp.bfloat16)


MESH = pl.DeviceIdType.MESH
OTHERS = (1, 3, 2)
VMEM_SPEC = pl.BlockSpec(memory_space=pltpu.VMEM)


def place():
    seq = lax.axis_index("seq")
    return seq // 8, (seq // 2) % 4, seq % 2


def seq_of(x, z, c):
    return (x * 4 + z) * 2 + c


def remote(source, target, send_sem, recv_sem, device):
    return pltpu.make_async_remote_copy(
        src_ref=source,
        dst_ref=target,
        send_sem=send_sem,
        recv_sem=recv_sem,
        device_id=device,
        device_id_type=MESH,
    )


def seq_peers():
    x, z, c = place()
    along_z = [{"seq": seq_of(x, (z + d) % 4, c)} for d in OTHERS]
    along_x = [{"seq": seq_of((x + d) % 4, z, c)} for d in OTHERS]
    return along_z + along_x + [{"seq": seq_of(x, z, 1 - c)}]


def tp_peers():
    tp = lax.axis_index("tp")
    return [{"tp": (tp + d) % 4} for d in OTHERS]


def chip_column_peers():
    x, z, c = place()
    pairs = [(dz, dc) for dz in (0,) + OTHERS for dc in (0, 1) if (dz, dc) != (0, 0)]
    return [{"seq": seq_of(x, (z + dz) % 4, (c + dc) % 2)} for dz, dc in pairs]


def plane_peers():
    x, z, c = place()
    tp = lax.axis_index("tp")
    pairs = [(dx, dt) for dx in (0,) + OTHERS for dt in (0,) + OTHERS if (dx, dt) != (0, 0)]
    return [{"seq": seq_of((x + dx) % 4, z, c), "tp": (tp + dt) % 4} for dx, dt in pairs]


def greet(peers):
    barrier = pltpu.get_barrier_semaphore()
    for peer in peers:
        pl.semaphore_signal(barrier, inc=1, device_id=peer, device_id_type=MESH)
    pl.semaphore_wait(barrier, len(peers))


class SeqGather:
    def __init__(self, own, blocks, send_sems, recv_sems):
        self.own, self.blocks = own, blocks
        self.send_sems, self.recv_sems = send_sems, recv_sems

    def send(self, slot, source, x, z, c, device):
        remote(
            source,
            self.blocks.at[x, z, c],
            self.send_sems.at[slot],
            self.recv_sems.at[x, z, c],
            device,
        ).start()

    def arrived(self, x, z, c):
        block = self.blocks.at[x, z, c]
        remote(
            block, block, self.send_sems.at[0], self.recv_sems.at[x, z, c], seq_peers()[-1]
        ).wait_recv()

    def start_z(self):
        x, z, c = place()
        for k, peer in enumerate(seq_peers()[:3]):
            self.send(k, self.own, x, z, c, peer)

    def start_x(self):
        x, z, c = place()
        for k, peer in enumerate(seq_peers()[3:]):
            self.send(3 + k, self.own, x, z, c, peer)

    def start(self):
        self.start_z()
        self.start_x()

    def forward_z(self):
        x, z, c = place()
        peers = seq_peers()
        for i, d in enumerate(OTHERS):
            from_z = (z + d) % 4
            self.arrived(x, from_z, c)
            for k, peer in enumerate(peers[3:]):
                self.send(7 + 4 * i + k, self.blocks.at[x, from_z, c], x, from_z, c, peer)

    def forward_x(self):
        x, z, c = place()
        partner = seq_peers()[-1]
        for i, dz in enumerate((0,) + OTHERS):
            for k, dx in enumerate(OTHERS):
                from_x, from_z = (x + dx) % 4, (z + dz) % 4
                self.arrived(from_x, from_z, c)
                block = self.blocks.at[from_x, from_z, c]
                self.send(19 + 3 * i + k, block, from_x, from_z, c, partner)

    def finish(self):
        x, z, c = place()
        for dz in (0,) + OTHERS:
            for dx in (0,) + OTHERS:
                self.arrived((x + dx) % 4, (z + dz) % 4, 1 - c)

    def drain(self):
        x, z, c = place()
        block = self.blocks.at[x, z, c]
        for slot in range(GATHER_SENDS):
            remote(
                block, block, self.send_sems.at[slot], self.recv_sems.at[x, z, c], seq_peers()[-1]
            ).wait_send()


GATHER_SENDS = 7 + 12 + 12


def head_norm_rope(values, gain, cosine, sine):
    lane = lax.broadcasted_iota(jnp.int32, (values.shape[0], 128), 1)
    low = lane < HEAD
    groups = []
    for g in range(values.shape[1] // 128):
        part = values[:, g * 128 : (g + 1) * 128]

        def average(t):
            first = jnp.sum(jnp.where(low, t, 0.0), axis=1, keepdims=True)
            second = jnp.sum(jnp.where(low, 0.0, t), axis=1, keepdims=True)
            return jnp.where(low, first, second) * (1.0 / HEAD)

        centred = part - average(part)
        unit = centred * lax.rsqrt(average(centred * centred) + 1e-06)
        unit = unit * gain
        turned = jnp.where(lane % 2 == 0, pltpu.roll(unit, 127, 1), pltpu.roll(unit, 1, 1))
        groups.append(unit * cosine + turned * sine)
    return jnp.concatenate(groups, axis=1)


def layer_kernel(
    hidden_ref,
    w_qkv_hbm,
    w_out_hbm,
    stale_ref,
    mod_ref,
    gain_ref,
    cos_ref,
    sin_ref,
    length_ref,
    out_ref,
    kv_ref,
    w_qkv,
    w_out,
    x_all,
    stale_all,
    fresh_keys,
    fresh_values,
    partial,
    reduced,
    mod_all,
    w_sems,
    x_send,
    x_recv,
    pass_send,
    r_send,
    r_recv,
    stale_send,
    stale_recv,
    key_send,
    key_recv,
    value_send,
    value_recv,
    mod_local,
    mod_send,
    column_recv,
    plane_recv,
):
    x, z, c = place()
    tp = lax.axis_index("tp")
    section = lax.axis_index("section")
    rows, share = hidden_ref.shape
    head_cols = w_qkv.shape[2]
    heads = head_cols // HEAD
    load_qkv = pltpu.make_async_copy(w_qkv_hbm, w_qkv, w_sems.at[0])
    load_out = pltpu.make_async_copy(w_out_hbm, w_out, w_sems.at[1])
    load_qkv.start()
    load_out.start()
    across = [{"section": 1 - section, "tp": (tp + d) % 4} for d in (0,) + OTHERS]
    greet(chip_column_peers() + plane_peers() + across)

    @pl.when(section == 0)
    def _():
        for k, peer in enumerate(tp_peers()):
            remote(hidden_ref, x_all.at[tp], x_send.at[k], x_recv.at[tp], peer).start()
        x_all[tp] = hidden_ref[...]

    keep = pltpu.make_async_copy(mod_ref, mod_all.at[x, tp, z, c], mod_local)
    keep.start()

    def column_copy(k, from_z, from_c):
        return remote(
            mod_ref,
            mod_all.at[x, tp, from_z, from_c],
            mod_send.at[k],
            column_recv.at[from_z, from_c],
            chip_column_peers()[k],
        )

    def plane_copy(k, from_x, from_tp):
        return remote(
            mod_all.at[from_x, from_tp],
            mod_all.at[from_x, from_tp],
            mod_send.at[7 + k],
            plane_recv.at[from_x, from_tp],
            plane_peers()[k],
        )

    for k in range(7):
        column_copy(k, z, c).start()
    stale = SeqGather(stale_ref, stale_all, stale_send, stale_recv)

    @pl.when(section == 0)
    def _():
        stale.start()

    stale_all[x, z, c] = stale_ref[...]
    keep.wait()
    for dz in (0,) + OTHERS:
        for dc in (0, 1):
            if (dz, dc) != (0, 0):
                column_copy(0, (z + dz) % 4, (c + dc) % 2).wait_recv()
    for k in range(15):
        plane_copy(k, x, tp).start()

    @pl.when(section == 0)
    def _():
        stale.forward_z()

    for dx in (0,) + OTHERS:
        for dt in (0,) + OTHERS:
            if (dx, dt) != (0, 0):
                plane_copy(0, (x + dx) % 4, (tp + dt) % 4).wait_recv()

    def x_arrived(source):
        remote(
            hidden_ref, x_all.at[source], x_send.at[0], x_recv.at[source], tp_peers()[0]
        ).wait_recv()

    @pl.when(section == 1)
    def _():
        stale.start()
        stale.forward_z()
        stale.forward_x()
        stale.finish()
        x_arrived(tp)

    for d in OTHERS:
        x_arrived((tp + d) % 4)

    token = lax.axis_index("seq") * rows + lax.broadcasted_iota(jnp.int32, (rows, 1), 0)
    video = token >= TEXT
    width = share * 4
    tiles = share // 128

    def mod_tile(row, index):
        group, step = divmod(row * (width // 128) + index, 9)
        found = None
        for member, half in ((step, 0), (step - 1, 1)):
            if 0 <= member < 8:
                at = (group // 4, member % 4, group % 4, member // 4, slice(half, half + 1))
                found = mod_all[at] if found is None else found + mod_all[at]
        return found

    def mod_rows(row, t):
        parts = [
            jnp.where(video, mod_tile(row, t * tiles + i), mod_tile(row + 3, t * tiles + i))
            for i in range(tiles)
        ]
        return jnp.concatenate(parts, axis=1)

    total = jnp.zeros((rows, 1), jnp.float32)
    for t in range(4):
        total += jnp.sum(x_all[t].astype(jnp.float32), axis=1, keepdims=True)
    mean = total * (1.0 / width)
    square = jnp.zeros((rows, 1), jnp.float32)
    for t in range(4):
        centred = x_all[t].astype(jnp.float32) - mean
        square += jnp.sum(centred * centred, axis=1, keepdims=True)
    inverse = lax.rsqrt(square * (1.0 / width) + 1e-05)
    load_qkv.wait()
    normed = []
    for t in range(4):
        centred = x_all[t].astype(jnp.float32) - mean
        scaled = centred * inverse * (1.0 + mod_rows(1, t)) + mod_rows(0, t)
        normed.append(scaled.astype(jnp.bfloat16))

    def project(part):
        proj = jnp.zeros((rows, head_cols), jnp.float32)
        for t in range(4):
            weights = w_qkv[part, t * share : (t + 1) * share, :]
            proj += jnp.dot(normed[t], weights, preferred_element_type=jnp.float32)
        return proj

    cosine, sine = cos_ref[...], sin_ref[...]
    gains = jnp.concatenate([gain_ref[...]] * 2, axis=1)
    keys = head_norm_rope(project(1), gains[1:2], cosine, sine).astype(jnp.bfloat16)
    kv_ref[0] = keys
    fresh_keys[x, z, c] = keys
    key_gather = SeqGather(kv_ref.at[0], fresh_keys, key_send, key_recv)
    key_gather.start()
    values = project(2).astype(jnp.bfloat16)
    kv_ref[1] = values
    fresh_values[x, z, c] = values
    value_gather = SeqGather(kv_ref.at[1], fresh_values, value_send, value_recv)
    value_gather.start()

    queries = head_norm_rope(project(0), gains[0:1], cosine, sine)
    stacked = jnp.concatenate([queries] * heads, axis=0)
    row_head = lax.broadcasted_iota(jnp.int32, stacked.shape, 0) // rows
    col_head = lax.broadcasted_iota(jnp.int32, stacked.shape, 1) // HEAD
    spread = jnp.where(row_head == col_head, stacked, 0.0).astype(jnp.bfloat16)
    key_gather.forward_z()
    value_gather.forward_z()

    @pl.when(section == 0)
    def _():
        stale.forward_x()

    key_gather.forward_x()

    @pl.when(section == 0)
    def _():
        stale.finish()

    tokens = rows * 32

    def all_rows(blocks):
        return blocks.reshape(tokens, head_cols)

    contract = (((1,), (1,)), ((), ()))
    scores_stale = lax.dot_general(
        spread, all_rows(stale_all[:, :, :, 0]), contract, preferred_element_type=jnp.float32
    )
    key_gather.finish()
    scores_fresh = lax.dot_general(
        spread, all_rows(fresh_keys[...]), contract, preferred_element_type=jnp.float32
    )
    column = lax.broadcasted_iota(jnp.int32, scores_fresh.shape, 1)
    first = TEXT + length_ref[0]
    second = first + length_ref[1]
    third = second + length_ref[2]
    limit = jnp.where(token < third, third, tokens)
    limit = jnp.where(token < first, first, jnp.where(token < second, second, limit))
    allowed = column < jnp.concatenate([limit] * heads, axis=0)
    scores = jnp.where(allowed, scores_fresh, scores_stale) * HEAD ** (-0.5)
    weights = jnp.exp(scores - jnp.max(scores, axis=1, keepdims=True))
    denominator = jnp.sum(weights, axis=1, keepdims=True)
    part_fresh = jnp.where(allowed, weights, 0.0).astype(jnp.bfloat16)
    part_stale = jnp.where(allowed, 0.0, weights).astype(jnp.bfloat16)
    value_gather.forward_x()
    mixed = jnp.dot(
        part_stale, all_rows(stale_all[:, :, :, 1]), preferred_element_type=jnp.float32
    )
    value_gather.finish()
    mixed += jnp.dot(part_fresh, all_rows(fresh_values[...]), preferred_element_type=jnp.float32)
    mixed = jnp.where(row_head == col_head, mixed / denominator, 0.0)
    attended = mixed[0:rows]
    for h in range(1, heads):
        attended += mixed[h * rows : (h + 1) * rows]
    attended = attended.astype(jnp.bfloat16)

    load_out.wait()
    for t in range(4):
        partial[t] = jnp.dot(
            attended, w_out[:, t * share : (t + 1) * share], preferred_element_type=jnp.float32
        ).astype(jnp.bfloat16)
    r_copies = []
    for k, d in enumerate(OTHERS):
        target = (tp + d) % 4
        copy = remote(
            partial.at[target], reduced.at[tp], r_send.at[k], r_recv.at[tp], {"tp": target}
        )
        copy.start()
        r_copies.append(copy)
    gate = jnp.zeros((rows, share), jnp.float32)
    for t in range(4):
        gate = jnp.where(tp == t, mod_rows(2, t), gate)
    projected = partial[tp].astype(jnp.float32)
    for k, d in enumerate(OTHERS):
        source = (tp + d) % 4
        remote(
            partial.at[source], reduced.at[source], r_send.at[k], r_recv.at[source], {"tp": source}
        ).wait_recv()
        projected += reduced[source].astype(jnp.float32)
    out_ref[...] = (x_all[tp].astype(jnp.float32) + gate * projected).astype(jnp.bfloat16)

    @pl.when(section == 0)
    def _():
        passes = []
        for k, peer in enumerate(across):
            copy = remote(out_ref, x_all.at[tp], pass_send.at[k], x_recv.at[tp], peer)
            copy.start()
            passes.append(copy)
        for k, peer in enumerate(tp_peers()):
            remote(hidden_ref, x_all.at[tp], x_send.at[k], x_recv.at[tp], peer).wait_send()
        for copy in passes:
            copy.wait_send()

    for copy in r_copies:
        copy.wait_send()
    for k in range(7):
        column_copy(k, z, c).wait_send()
    for k in range(15):
        plane_copy(k, x, tp).wait_send()
    stale.drain()
    key_gather.drain()
    value_gather.drain()


def run_layers(hidden, w_qkv, w_out, stale, modulate, gains, cosine, sine, lengths):
    rows, share = hidden.shape
    head_cols = w_out.shape[0]
    blocks = pltpu.VMEM((4, 4, 2, 2, rows, head_cols), jnp.bfloat16)
    half_blocks = pltpu.VMEM((4, 4, 2, rows, head_cols), jnp.bfloat16)
    dma = pltpu.SemaphoreType.DMA
    any_spec = pl.BlockSpec(memory_space=pl.ANY)
    return pl.pallas_call(
        layer_kernel,
        out_shape=(
            jax.ShapeDtypeStruct((rows, share), jnp.bfloat16),
            jax.ShapeDtypeStruct((2, rows, head_cols), jnp.bfloat16),
        ),
        in_specs=[VMEM_SPEC, any_spec, any_spec]
        + [VMEM_SPEC] * 5
        + [pl.BlockSpec(memory_space=pltpu.SMEM)],
        out_specs=(VMEM_SPEC, VMEM_SPEC),
        scratch_shapes=[
            pltpu.VMEM(w_qkv.shape, jnp.bfloat16),
            pltpu.VMEM(w_out.shape, jnp.bfloat16),
            pltpu.VMEM((4, rows, share), jnp.bfloat16),
            blocks,
            half_blocks,
            half_blocks,
            pltpu.VMEM((4, rows, share), jnp.bfloat16),
            pltpu.VMEM((4, rows, share), jnp.bfloat16),
            pltpu.VMEM((4, 4, 4, 2, 2, 128), jnp.float32),
            dma((2,)),
            dma((3,)),
            dma((4,)),
            dma((4,)),
            dma((3,)),
            dma((4,)),
            dma((GATHER_SENDS,)),
            dma((4, 4, 2)),
            dma((GATHER_SENDS,)),
            dma((4, 4, 2)),
            dma((GATHER_SENDS,)),
            dma((4, 4, 2)),
            dma,
            dma((22,)),
            dma((4, 2)),
            dma((4, 4)),
        ],
        compiler_params=pltpu.CompilerParams(collective_id=0, has_side_effects=True),
    )(hidden, w_qkv, w_out, stale, modulate, gains, cosine, sine, lengths)


def rope_tables(positions, first_row):
    column = jnp.arange(128)
    pair = (column % HEAD) // 2
    spans = ((0, HEAD // 4), (HEAD // 8, 3 * HEAD // 8), (5 * HEAD // 16, 3 * HEAD // 8))
    coords = positions.astype(jnp.float32)
    angles = jnp.zeros((positions.shape[1], 128), jnp.float32)
    for axis, (start, size) in enumerate(spans):
        exponent = 2.0 * (pair - start).astype(jnp.float32) / size
        inside = (pair >= start) & (pair < start + size // 2)
        frequency = jnp.where(inside, 1.0 / 10000.0**exponent, 0.0)
        angles = angles + coords[axis][:, None] * frequency[None, :]
    video = (first_row + jnp.arange(positions.shape[1]) >= TEXT)[:, None]
    sign = jnp.where(column % 2 == 0, -1.0, 1.0)[None, :]
    cosine = jnp.where(video, jnp.cos(angles), 1.0)
    return cosine, jnp.where(video, jnp.sin(angles) * sign, 0.0)


def local(
    hidden,
    qkv_weight,
    qk_gain,
    out_weight,
    mod_weight,
    stale_kv,
    patch_lengths,
    positions,
    timestep,
):
    tok_rows = hidden.shape[0]
    seq_rank = lax.axis_index("seq")
    share = jnp.dot(time_features(timestep), mod_weight[0], preferred_element_type=jnp.float32)
    device = seq_rank * lax.axis_size("tp") + lax.axis_index("tp")
    offset = (share.shape[1] * device) % 128
    placed = lax.dynamic_update_slice(jnp.zeros((1, 256), jnp.float32), share, (0, offset))
    cosine, sine = rope_tables(positions, seq_rank * tok_rows)
    result, fresh_kv = run_layers(
        hidden,
        jnp.transpose(qkv_weight[0], (1, 0, 2)),
        out_weight[0],
        stale_kv[0],
        placed.reshape(2, 128),
        qk_gain[0],
        cosine,
        sine,
        patch_lengths,
    )
    return (result[None], fresh_kv[None])


def solution(mesh):
    return jax.shard_map(
        local,
        mesh=mesh,
        in_specs=(
            P("seq", "tp"),
            P("section", None, None, "tp"),
            P("section", None, None),
            P("section", "tp", None),
            P("section", None, ("seq", "tp")),
            P("section", None, "seq", "tp"),
            P(),
            P(None, "seq"),
            P(),
        ),
        out_specs=(P("section", "seq", "tp"), P("section", None, "seq", "tp")),
        check_vma=False,
    )
```
